128 devices in a mesh: comp: 2 (over core), tile: 64 (over z, y, x).
Axes of the slice: x: 4, y: 4, z: 4, core: 2. Of those that a mesh axis runs over, the one named last changes fastest.
Arguments:
- state: float32 [2, 8, 1024, 1024], P('comp', None, 'tile'), may hold values from -80 to 80, as said below
- basis: bfloat16 [12, 2, 8, 1024, 1024], P(None, 'comp', None, 'tile'), may hold values from -4 to 4
- kappa: float32 [2, 1024, 1024], P('comp', 'tile'), may hold values from 0.05 to 0.22
- vmix: float32 [2, 8, 8], P('comp'), may hold values from -1 to 1
- land_mask: int32 [1024, 1024], P('tile'), may hold values 0 or 1
- send_rows: int32 [2, 64, 64, 8], P('comp', 'tile'), may hold values from 0 to 127
- recv_slots: int32 [2, 64, 128, 4], P('comp', 'tile'), may hold values from 0 to 511
- recv_weights: float32 [2, 64, 128, 4], P('comp', 'tile'), may hold values from 0.1 to 0.4
Outputs:
- direction: float32 [2, 8, 1024, 1024], P('comp', None, 'tile')
- coefs: float32 [12], replicated
The draws below stay inside these ranges and needn't reach their ends.
Inputs may be any that keep to these rules, and one draw needn't show every extreme that they name: `state`: the perturbation is noise plus a combination of the basis vectors.
All inputs are finite; a program needn't handle non-finite values. No bound on the sum of `land_mask` on one device may be relied on, other than what follows from the above.
Results may differ from the reference program's by a relative error of at most 0.0003.
Values sent between devices are 32-bit elements; how exact they have to be, the bound alone decides.
A program may use at most 64 MiB of HBM per device.

```python
import jax
import jax.numpy as jnp
from jax import lax

LEV = 8
COLS = 1024
FLUX = 4
OVER = 4
CAP = 8
VECS = 12
TILES = 64
ROWS = 1024
NB = 128


def basis_field(key):
    inner = jax.random.fold_in(key, 7)
    return jnp.clip(jax.random.normal(inner, (VECS, 2, LEV, ROWS, COLS), jnp.float32), -4.0, 4.0)


def draw_basis(key, part):
    return basis_field(key).astype(jnp.bfloat16)


def draw_state(key, part):
    qvals = basis_field(key).astype(jnp.bfloat16).astype(jnp.float32)
    amps = jax.random.uniform(jax.random.fold_in(key, 11), (VECS,), jnp.float32, -1.5, 1.5)
    noise = jnp.clip(jax.random.normal(jax.random.fold_in(key, 13), (2, LEV, ROWS, COLS), jnp.float32), -4.0, 4.0)
    mixed = 0.5 * noise
    for index in range(VECS):
        mixed = mixed + amps[index] * qvals[index]
    return mixed


def plant(array, own_key, low, largest):
    dims = array.shape
    spot = [jax.random.randint(jax.random.fold_in(own_key, axis), (), 0, dims[axis]) for axis in range(len(dims))]
    array = array.at[tuple(spot)].set(low)
    longest = dims.index(max(dims))
    spot[longest] = (spot[longest] + 1) % dims[longest]
    return array.at[tuple(spot)].set(largest)


def shard_levels(rng, shape, shards, least, top_value):
    loudness, own = 1.0, jax.random.fold_in(rng, 6)
    for dim, blocks in shards:
        draws = jnp.exp(jax.random.uniform(jax.random.fold_in(own, dim), (blocks,), jnp.float32, least / len(shards), top_value / len(shards)))
        loudness = loudness * jnp.repeat(draws, shape[dim] // blocks).reshape([-1 if axis == dim else 1 for axis in range(len(shape))])
    return loudness


def bell_draw(rng, shape, deviation, reach, cuts=(), kind=jnp.bfloat16):
    result = deviation * jax.random.normal(rng, shape, jnp.float32)
    if cuts:
        result = result * shard_levels(rng, shape, cuts, -0.22, 0.18)
    return jnp.clip(result, -reach, reach).astype(kind)


def setup_inputs(seed: int = 0) -> dict:
    key_list = jax.random.split(jax.random.key(seed), 9)
    state = draw_state(jax.random.fold_in(key_list[8], 71), 0)
    basis = draw_basis(jax.random.fold_in(key_list[8], 71), 0)
    kappa = jnp.clip(0.05 + 0.17 * jax.random.uniform(key_list[2], (2, ROWS, COLS), jnp.float32) ** shard_levels(key_list[2], (2, ROWS, COLS), ((0, 2), (1, 64)), -0.2, 0.2), 0.05, 0.22)
    vmix = bell_draw(key_list[3], (2, LEV, LEV), (4 * LEV) ** -0.5, 1.0, ((0, 2),), jnp.float32)
    land_mask = plant((jax.random.randint(key_list[4], (ROWS, COLS), 0, 4) < 3).astype(jnp.int32), jax.random.fold_in(key_list[4], 1), 0, 1)
    send_rows = plant(jax.random.randint(key_list[5], (2, TILES, TILES, CAP), 0, NB), jax.random.fold_in(key_list[5], 1), 0, NB - 1).astype(jnp.int32)
    recv_slots = plant(jax.random.randint(key_list[6], (2, TILES, NB, OVER), 0, TILES * CAP), jax.random.fold_in(key_list[6], 1), 0, (TILES * CAP) - 1).astype(jnp.int32)
    recv_weights = jnp.clip(0.1 + 0.3 * jax.random.uniform(key_list[7], (2, TILES, NB, OVER), jnp.float32) ** shard_levels(key_list[7], (2, TILES, NB, OVER), ((0, 2), (1, 64)), -0.2, 0.2), 0.1, 0.4)
    return {"state": state, "basis": basis, "kappa": kappa, "vmix": vmix, "land_mask": land_mask, "send_rows": send_rows, "recv_slots": recv_slots, "recv_weights": recv_weights}


def advance(x, kap, vert_mat, maskf, forced):
    padded = jnp.pad(x, ((0, 0), (0, 0), (1, 1), (0, 0)))
    lap = padded[:, :, 2:] + padded[:, :, :-2] + jnp.roll(x, 1, -1) + jnp.roll(x, -1, -1) - 4.0 * x
    vert = jnp.einsum('clm,cmrq->clrq', vert_mat, x, precision=lax.Precision.HIGHEST)
    return maskf[:, None] * (x + kap[:, None] * lap + vert + forced)

def reference(state, basis, kappa, vmix, land_mask, send_rows, recv_slots, recv_weights):
    surface = state[:, :FLUX].reshape(2, FLUX, TILES, NB, 128)
    band_ids = jnp.arange(TILES, dtype=jnp.int32)
    imports = []
    for recv in range(2):
        send = 1 - recv
        src = surface[send]

        def one(dest):
            rows_idx = send_rows[send][:, dest, :]
            buf = src[:, band_ids[:, None], rows_idx]
            flat = buf.reshape(FLUX, TILES * CAP, 128)
            picked = flat[:, recv_slots[recv, dest]]
            return jnp.einsum('ek,fekq->feq', recv_weights[recv, dest], picked, precision=lax.Precision.HIGHEST)
        per_band = lax.map(one, band_ids)
        imports.append(jnp.transpose(per_band, (1, 0, 2, 3)).reshape(FLUX, ROWS, COLS))
    imports = jnp.stack(imports)
    forced = jnp.concatenate([imports, jnp.zeros((2, LEV - FLUX, ROWS, COLS), jnp.float32)], 1)
    maskf = jnp.stack([land_mask.astype(jnp.float32), jnp.ones((ROWS, COLS), jnp.float32)])
    x = state
    for step in range(2):
        x = advance(x, kappa, vmix, maskf, forced)
    total = 2 * LEV * ROWS * COLS
    vflat = x.reshape(-1)
    qmat = basis.reshape(VECS, -1).astype(jnp.float32)
    coefs = jnp.dot(qmat, vflat, precision=lax.Precision.HIGHEST) / total
    remain = vflat - jnp.dot(coefs, qmat, precision=lax.Precision.HIGHEST)
    normsq = jnp.sum(remain * remain)
    direction = remain / jnp.sqrt(normsq / total + 1e-06)
    return (direction.reshape(2, LEV, ROWS, COLS), coefs)
```

```python
import functools

import jax
import jax.numpy as jnp
from jax import lax
from jax.experimental import pallas as pl
from jax.experimental.pallas import tpu as pltpu
from jax.sharding import PartitionSpec as P

FLUX = 4
VECS = 12
LEV = 8
ROWS = 16
COLS = 1024
TILES = 64
CAP = 8
NB = 128
GROUPS = 4
PER = TILES // GROUPS
MESH = pl.DeviceIdType.MESH
F32 = jnp.float32
BF16 = jnp.bfloat16
PAIRS = [(i, j) for i in range(VECS) for j in range(i, VECS)]


def hops(k):
    return sum((0, 1, 2, 1)[(k >> s) & 3] for s in (0, 2, 4))


PEERS = [sorted((k for k in range(1, TILES) if k & 1 == c), key=lambda k: -hops(k)) for c in (0, 1)]


def offset_of(step):
    a, b, c = step & 3, (step >> 2) & 3, step >> 4
    return a, (a + b) & 3, (a + c) & 3


def moved_tile(tile, step):
    dx, dy, dz = offset_of(step)
    return ((tile & 3) + dx & 3) | (((tile >> 2 & 3) + dy & 3) << 2) | (((tile >> 4) + dz & 3) << 4)


def remote(src, dst, send, recv, comp, tile):
    return pltpu.make_async_remote_copy(
        src_ref=src, dst_ref=dst, send_sem=send, recv_sem=recv, device_id=(comp, tile), device_id_type=MESH
    )


def wait_bytes(ref, sem):
    pltpu.make_async_copy(ref, ref, sem).wait()


def sum_over_devices(comp, tile, mine, pair, wide, part, other, sems):
    first = remote(mine, pair, sems.at[0], sems.at[1], 1 - comp, tile)
    first.start()
    first.wait()
    chip = mine[...] + pair[...]
    part[...] = chip
    odd = tile & 1
    slot = tile >> 1

    for c in (0, 1):

        @pl.when(comp == c)
        def _():
            for k in PEERS[c]:
                remote(part, wide.at[slot], sems.at[2], sems.at[3], odd, tile ^ k).start()

    @pl.when(comp == odd)
    def _():
        wide[slot] = chip
        wait_bytes(wide.at[pl.ds(0, TILES // 2 - 1)], sems.at[3])

    @pl.when(comp != odd)
    def _():
        wait_bytes(wide.at[pl.ds(0, TILES // 2)], sems.at[3])

    half = wide[0]
    for s in range(1, TILES // 2):
        half = half + wide[s]
    for c in (0, 1):

        @pl.when(comp == c)
        def _():
            wait_bytes(wide.at[pl.ds(0, len(PEERS[c]))], sems.at[2])

    part[...] = half
    last = remote(part, other, sems.at[4], sems.at[5], 1 - comp, tile)
    last.start()
    last.wait()
    return half + other[...]


def stencil(ref, level, kap):
    x = ref[level, 8:24, :]
    lap = (
        ref[level, 7:23, :]
        + ref[level, 9:25, :]
        + pltpu.roll(x, 1, 1)
        + pltpu.roll(x, COLS - 1, 1)
        - 4.0 * x
    )
    return x + kap * lap


def mixed(ref, vmix, level, count):
    total = vmix[0, level, 0] * ref[0, 8:24, :]
    for m in range(1, count):
        total = total + vmix[0, level, m] * ref[m, 8:24, :]
    return total


def kernel(
    state, basis, kappa, land, slots, weights, vmix, rows, direction, coefs,
    x0, x1, y, fh, f, basis_v, kap, land_v, maskf, surf, bucket, arrived, imp,
    g_mine, g_pair, g_wide, g_part, g_other, e_mine, e_pair, e_wide, e_part, e_other,
    load, send, recv, halo, gsem, esem, store,
):
    comp = lax.axis_index("comp")
    tile = lax.axis_index("tile")
    total = float(LEV * ROWS * COLS * TILES * 2)
    above = tile - 1 & TILES - 1
    below = tile + 1 & TILES - 1

    surf_loads = [
        pltpu.make_async_copy(
            state.at[0, pl.ds(0, FLUX), :, pl.ds(128 * j, 128)], surf.at[j], load.at[0]
        )
        for j in range(8)
    ]
    for c in surf_loads:
        c.start()
    x_load = pltpu.make_async_copy(state.at[0], x0.at[:, pl.ds(8, ROWS), :], load.at[1])
    x_load.start()
    barrier = pltpu.get_barrier_semaphore()

    def greet(step, carry):
        pl.semaphore_signal(barrier, inc=1, device_id=(1 - comp, moved_tile(tile, step)), device_id_type=MESH)
        return carry

    lax.fori_loop(0, TILES, greet, 0)
    for t in (above, below):
        pl.semaphore_signal(barrier, inc=1, device_id=(comp, t), device_id_type=MESH)
    kap_load = pltpu.make_async_copy(kappa.at[0], kap, load.at[2])
    kap_load.start()
    land_load = pltpu.make_async_copy(land, land_v, load.at[3])
    land_load.start()
    basis_load = pltpu.make_async_copy(basis.at[:, 0], basis_v, load.at[4])
    basis_load.start()
    for c in surf_loads:
        c.wait()
    x_load.wait()
    pl.semaphore_wait(barrier, TILES + 2)

    def swap_rows(ref, sems):
        up = remote(ref.at[:, pl.ds(8, 1), :], ref.at[:, pl.ds(24, 1), :], sems.at[0], sems.at[1], comp, above)
        down = remote(ref.at[:, pl.ds(23, 1), :], ref.at[:, pl.ds(7, 1), :], sems.at[2], sems.at[3], comp, below)
        up.start()
        down.start()
        return up, down

    def clear_ends(ref):
        n = ref.shape[0]

        @pl.when(tile == 0)
        def _():
            ref[:, 7:8, :] = jnp.zeros((n, 1, COLS), F32)

        @pl.when(tile == TILES - 1)
        def _():
            ref[:, 24:25, :] = jnp.zeros((n, 1, COLS), F32)

    swap0 = swap_rows(x0, halo.at[0])

    flat_surf = surf.reshape(8 * FLUX * ROWS, 128)
    flat_bucket = bucket.reshape(TILES * FLUX * CAP, 128)

    def deliver(step, carry):
        dest = moved_tile(tile, step)
        for j in range(CAP):
            blk = rows[0, 0, dest, j]
            start = (blk & 7) * (FLUX * ROWS) + (blk >> 3)
            flat_bucket[pl.ds(step * (FLUX * CAP) + j, FLUX, stride=CAP), :] = flat_surf[
                pl.ds(start, FLUX, stride=ROWS), :
            ]
        remote(bucket.at[step], arrived.at[step], send, recv.at[step >> 4], 1 - comp, dest).start()
        return carry

    lax.fori_loop(0, TILES, deliver, 0)

    basis_load.wait()
    lane = lax.broadcasted_iota(jnp.int32, (16, 128), 1)
    sub = lax.broadcasted_iota(jnp.int32, (16, 128), 0)
    rows_of = {}
    third = len(PAIRS) // 3
    for part in range(3):
        pairs = PAIRS[part * third : (part + 1) * third]

        def gram_step(n, acc, pairs=pairs):
            level = n >> 3
            at = pl.multiple_of((n & 7) * 128, 128)
            used = sorted({i for p in pairs for i in p})
            vals = {i: basis_v[i, level, :, pl.ds(at, 128)].astype(F32) for i in used}
            out = []
            for (i, j), a in zip(pairs, acc):
                p = vals[i] * vals[j]
                out.append(a + (p[:8] + p[8:]))
            return tuple(out)

        acc = lax.fori_loop(0, 64, gram_step, tuple(jnp.zeros((8, 128), F32) for _ in pairs))
        for p, a in zip(pairs, acc):
            rows_of[p] = jnp.sum(a, axis=0, keepdims=True)
    gram_here = jnp.zeros((16, 128), F32)
    for i in range(VECS):
        stack = jnp.concatenate(
            [rows_of[(min(i, j), max(i, j))] for j in range(VECS)] + [jnp.zeros((4, 128), F32)], axis=0
        )
        gram_here = jnp.where(lane == i, jnp.sum(stack, axis=1, keepdims=True), gram_here)
    g_mine[...] = gram_here

    kap_load.wait()
    land_load.wait()
    maskf[...] = jnp.where(comp == 0, land_v[...].astype(F32), jnp.ones((ROWS, COLS), F32))
    for c in swap0:
        c.wait()
    clear_ends(x0)
    for l in range(LEV):
        x1[l, 8:24, :] = maskf[...] * (stencil(x0, l, kap[...]) + mixed(x0, vmix, l, LEV))
    swap1 = swap_rows(x1, halo.at[1])
    gram = sum_over_devices(comp, tile, g_mine, g_pair, g_wide, g_part, g_other, gsem)
    for c in swap1:
        c.wait()
    clear_ends(x1)
    for l in range(LEV):
        y[l] = maskf[...] * (stencil(x1, l, kap[...]) + mixed(x1, vmix, l, LEV))

    slot = slots[0, 0]
    weight = weights[0, 0]
    src = slot >> 3
    a = (tile & 3) - (src & 3) & 3
    b = (tile >> 2 & 3) - (src >> 2 & 3) - a & 3
    c = (tile >> 4) - (src >> 4) - a & 3
    place = (a | b << 2 | c << 4) * CAP + (slot & 7)
    at_lane = lax.broadcasted_iota(jnp.int32, (NB, TILES * CAP), 1)
    matrix = jnp.zeros((NB, TILES * CAP), F32)
    for k in range(4):
        matrix = matrix + jnp.where(at_lane == place[:, k : k + 1], weight[:, k : k + 1], 0.0)
    high = matrix.astype(BF16)
    low = (matrix - high.astype(F32)).astype(BF16)
    dot = functools.partial(jnp.dot, preferred_element_type=F32)
    sums = jnp.zeros((NB, FLUX * 128), F32)
    for g in range(GROUPS):
        wait_bytes(arrived.at[pl.ds(g * PER, PER)], recv.at[g])
        got = jnp.concatenate(
            [arrived[g * PER : (g + 1) * PER, i].reshape(PER * CAP, 128) for i in range(FLUX)], axis=1
        )
        got_high = got.astype(BF16)
        got_low = (got - got_high.astype(F32)).astype(BF16)
        cut = slice(g * PER * CAP, (g + 1) * PER * CAP)
        sums = sums + dot(high[:, cut], got_high) + dot(low[:, cut], got_high) + dot(high[:, cut], got_low)
    for i in range(FLUX):
        imp[i * NB : (i + 1) * NB, :] = sums[:, i * 128 : (i + 1) * 128]
    for i in range(FLUX):
        for j in range(8):
            piece = imp[pl.ds(i * NB + j, ROWS, stride=8), :]
            f[i, :, j * 128 : (j + 1) * 128] = piece
            fh[i, 8:24, j * 128 : (j + 1) * 128] = maskf[:, j * 128 : (j + 1) * 128] * piece
    swap2 = swap_rows(fh, halo.at[2])
    for c in swap2:
        c.wait()
    clear_ends(fh)
    for l in range(LEV):
        z = mixed(fh, vmix, l, FLUX)
        if l < FLUX:
            z = z + stencil(fh, l, kap[...]) + f[l]
        y[l] = y[l] + maskf[...] * z

    def dot_step(n, acc):
        level = n >> 3
        at = pl.multiple_of((n & 7) * 128, 128)
        x = y[level, :, pl.ds(at, 128)]
        out = [a + basis_v[i, level, :, pl.ds(at, 128)].astype(F32) * x for i, a in enumerate(acc[:VECS])]
        return tuple(out) + (acc[VECS] + x * x,)

    acc = lax.fori_loop(0, 64, dot_step, tuple(jnp.zeros((16, 128), F32) for _ in range(VECS + 1)))
    stack = jnp.concatenate([jnp.sum(a, axis=0, keepdims=True) for a in acc] + [jnp.zeros((3, 128), F32)], axis=0)
    col = jnp.sum(stack, axis=1, keepdims=True)
    e_mine[...] = jnp.sum(jnp.where(lane == sub, col, 0.0), axis=0, keepdims=True)
    dots = sum_over_devices(comp, tile, e_mine, e_pair, e_wide, e_part, e_other, esem)
    first = lax.broadcasted_iota(jnp.int32, (1, 128), 1)
    coef = jnp.where(first < VECS, dots * (1.0 / total), 0.0)
    coefs[...] = coef
    coef_col = jnp.sum(jnp.where(lane == sub, jnp.broadcast_to(coef, (16, 128)), 0.0), axis=1, keepdims=True)
    square = jnp.sum(jnp.where(first == VECS, dots, 0.0) - 2.0 * dots * coef, axis=1, keepdims=True)
    gc = jnp.sum(gram * coef, axis=1, keepdims=True)
    square = square + jnp.sum(gc * coef_col, axis=0, keepdims=True)
    scale = 1.0 / jnp.sqrt(jnp.maximum(square, 0.0) * (1.0 / total) + 1e-06)
    weigh = [jnp.broadcast_to(coef_col[i : i + 1] * scale, (16, 128)) for i in range(VECS)]
    scale = jnp.broadcast_to(scale, (16, 128))

    for l in range(LEV):

        def finish(n, carry):
            at = pl.multiple_of(n * 128, 128)
            w = scale * y[l, :, pl.ds(at, 128)]
            for i in range(VECS):
                w = w - weigh[i] * basis_v[i, l, :, pl.ds(at, 128)].astype(F32)
            y[l, :, pl.ds(at, 128)] = w
            return carry

        lax.fori_loop(0, 8, finish, 0)
        pltpu.make_async_copy(y.at[l], direction.at[0, l], store).start()
    wait_bytes(bucket, send)
    wait_bytes(y, store)


def body(state, basis, kappa, vmix, land_mask, send_rows, recv_slots, recv_weights):
    anywhere = pl.BlockSpec(memory_space=pl.ANY)
    vmem = pl.BlockSpec(memory_space=pltpu.VMEM)
    smem = pl.BlockSpec(memory_space=pltpu.SMEM)
    dma = pltpu.SemaphoreType.DMA
    pad = (LEV, 32, COLS)
    direction, coefs = pl.pallas_call(
        kernel,
        out_shape=(
            jax.ShapeDtypeStruct((1, LEV, ROWS, COLS), F32),
            jax.ShapeDtypeStruct((1, 128), F32),
        ),
        in_specs=[anywhere, anywhere, anywhere, anywhere, vmem, vmem, smem, smem],
        out_specs=(anywhere, vmem),
        scratch_shapes=[
            pltpu.VMEM(pad, F32),
            pltpu.VMEM(pad, F32),
            pltpu.VMEM((LEV, ROWS, COLS), F32),
            pltpu.VMEM((FLUX, 32, COLS), F32),
            pltpu.VMEM((FLUX, ROWS, COLS), F32),
            pltpu.VMEM((VECS, LEV, ROWS, COLS), BF16),
            pltpu.VMEM((ROWS, COLS), F32),
            pltpu.VMEM((ROWS, COLS), jnp.int32),
            pltpu.VMEM((ROWS, COLS), F32),
            pltpu.VMEM((8, FLUX, ROWS, 128), F32),
            pltpu.VMEM((TILES, FLUX, CAP, 128), F32),
            pltpu.VMEM((TILES, FLUX, CAP, 128), F32),
            pltpu.VMEM((FLUX * NB, 128), F32),
            pltpu.VMEM((16, 128), F32),
            pltpu.VMEM((16, 128), F32),
            pltpu.VMEM((TILES // 2, 16, 128), F32),
            pltpu.VMEM((16, 128), F32),
            pltpu.VMEM((16, 128), F32),
            pltpu.VMEM((1, 128), F32),
            pltpu.VMEM((1, 128), F32),
            pltpu.VMEM((TILES // 2, 1, 128), F32),
            pltpu.VMEM((1, 128), F32),
            pltpu.VMEM((1, 128), F32),
            dma((5,)),
            dma(()),
            dma((GROUPS,)),
            dma((3, 4)),
            dma((6,)),
            dma((6,)),
            dma(()),
        ],
        compiler_params=pltpu.CompilerParams(
            collective_id=0, has_side_effects=True, vmem_limit_bytes=56 << 20
        ),
        name="interval",
    )(state, basis, kappa, land_mask, recv_slots, recv_weights, vmix, send_rows)
    return direction, coefs[0, :VECS]


def solution(mesh):
    return jax.shard_map(
        body,
        mesh=mesh,
        in_specs=(
            P("comp", None, "tile", None),
            P(None, "comp", None, "tile", None),
            P("comp", "tile", None),
            P("comp", None, None),
            P("tile", None),
            P("comp", "tile", None, None),
            P("comp", "tile", None, None),
            P("comp", "tile", None, None),
        ),
        out_specs=(P("comp", None, "tile", None), P()),
        check_vma=False,
    )
```

```python
import functools

import jax
import jax.numpy as jnp
from jax import lax
from jax.experimental import pallas as pl
from jax.experimental.pallas import tpu as pltpu
from jax.sharding import PartitionSpec as P

FLUX = 4
VECS = 12
LEV = 8
ROWS = 16
COLS = 1024
TILES = 64
CAP = 8
NB = 128
GROUPS = 4
PER = TILES // GROUPS
MESH = pl.DeviceIdType.MESH
F32 = jnp.float32
BF16 = jnp.bfloat16
PAIRS = [(i, j) for i in range(VECS) for j in range(i, VECS)]


def hops(k):
    return sum((0, 1, 2, 1)[(k >> s) & 3] for s in (0, 2, 4))


PEERS = [sorted((k for k in range(1, TILES) if k & 1 == c), key=lambda k: -hops(k)) for c in (0, 1)]


def offset_of(step):
    a, b, c = step & 3, (step >> 2) & 3, step >> 4
    return a, (a + b) & 3, (a + c) & 3


def moved_tile(tile, step):
    dx, dy, dz = offset_of(step)
    return ((tile & 3) + dx & 3) | (((tile >> 2 & 3) + dy & 3) << 2) | (((tile >> 4) + dz & 3) << 4)


def remote(src, dst, send, recv, comp, tile):
    return pltpu.make_async_remote_copy(
        src_ref=src, dst_ref=dst, send_sem=send, recv_sem=recv, device_id=(comp, tile), device_id_type=MESH
    )


def wait_bytes(ref, sem):
    pltpu.make_async_copy(ref, ref, sem).wait()


def sum_over_devices(comp, tile, mine, pair, wide, part, other, sems):
    first = remote(mine, pair, sems.at[0], sems.at[1], 1 - comp, tile)
    first.start()
    first.wait()
    chip = mine[...] + pair[...]
    part[...] = chip
    odd = tile & 1
    slot = tile >> 1

    for c in (0, 1):

        @pl.when(comp == c)
        def _():
            for k in PEERS[c]:
                remote(part, wide.at[slot], sems.at[2], sems.at[3], odd, tile ^ k).start()

    @pl.when(comp == odd)
    def _():
        wide[slot] = chip
        wait_bytes(wide.at[pl.ds(0, TILES // 2 - 1)], sems.at[3])

    @pl.when(comp != odd)
    def _():
        wait_bytes(wide.at[pl.ds(0, TILES // 2)], sems.at[3])

    half = wide[0]
    for s in range(1, TILES // 2):
        half = half + wide[s]
    for c in (0, 1):

        @pl.when(comp == c)
        def _():
            wait_bytes(wide.at[pl.ds(0, len(PEERS[c]))], sems.at[2])

    part[...] = half
    last = remote(part, other, sems.at[4], sems.at[5], 1 - comp, tile)
    last.start()
    last.wait()
    return half + other[...]


def stencil(ref, level, kap):
    x = ref[level, 8:24, :]
    lap = (
        ref[level, 7:23, :]
        + ref[level, 9:25, :]
        + pltpu.roll(x, 1, 1)
        + pltpu.roll(x, COLS - 1, 1)
        - 4.0 * x
    )
    return x + kap * lap


def mixed(ref, vmix, level, count):
    total = vmix[level, 0] * ref[0, 8:24, :]
    for m in range(1, count):
        total = total + vmix[level, m] * ref[m, 8:24, :]
    return total


def kernel(
    state, basis, kappa, land, slots_hbm, weights_hbm, vmix_hbm, rows_hbm, direction, coefs,
    slots, weights, vmix, rows, x0, x1, y, fh, f, basis_v, kap, land_v, maskf, surf, bucket, arrived, imp,
    g_mine, g_pair, g_wide, g_part, g_other, e_mine, e_pair, e_wide, e_part, e_other,
    load, send, recv, halo, gsem, esem,
):
    comp = lax.axis_index("comp")
    tile = lax.axis_index("tile")
    total = float(LEV * ROWS * COLS * TILES * 2)
    above = tile - 1 & TILES - 1
    below = tile + 1 & TILES - 1

    surf_loads = [
        pltpu.make_async_copy(
            state.at[0, pl.ds(0, FLUX), :, pl.ds(128 * j, 128)], surf.at[j], load.at[0]
        )
        for j in range(8)
    ]
    for c in surf_loads:
        c.start()
    rows_load = pltpu.make_async_copy(rows_hbm.at[0, 0], rows, load.at[5])
    rows_load.start()
    x_load = pltpu.make_async_copy(state.at[0], x0.at[:, pl.ds(8, ROWS), :], load.at[1])
    x_load.start()
    barrier = pltpu.get_barrier_semaphore()

    def greet(step, carry):
        pl.semaphore_signal(barrier, inc=1, device_id=(1 - comp, moved_tile(tile, step)), device_id_type=MESH)
        return carry

    lax.fori_loop(0, TILES, greet, 0)
    for t in (above, below):
        pl.semaphore_signal(barrier, inc=1, device_id=(comp, t), device_id_type=MESH)
    kap_load = pltpu.make_async_copy(kappa.at[0], kap, load.at[2])
    kap_load.start()
    land_load = pltpu.make_async_copy(land, land_v, load.at[3])
    land_load.start()
    vmix_load = pltpu.make_async_copy(vmix_hbm.at[0], vmix, load.at[6])
    vmix_load.start()
    table_loads = [
        pltpu.make_async_copy(slots_hbm.at[0, 0], slots, load.at[7]),
        pltpu.make_async_copy(weights_hbm.at[0, 0], weights, load.at[8]),
    ]
    for c in table_loads:
        c.start()
    basis_load = pltpu.make_async_copy(basis.at[:, 0], basis_v, load.at[4])
    basis_load.start()
    for c in surf_loads:
        c.wait()
    rows_load.wait()
    x_load.wait()
    pl.semaphore_wait(barrier, TILES + 2)

    def swap_rows(ref, sems):
        up = remote(ref.at[:, pl.ds(8, 1), :], ref.at[:, pl.ds(24, 1), :], sems.at[0], sems.at[1], comp, above)
        down = remote(ref.at[:, pl.ds(23, 1), :], ref.at[:, pl.ds(7, 1), :], sems.at[2], sems.at[3], comp, below)
        up.start()
        down.start()
        return up, down

    def clear_ends(ref):
        n = ref.shape[0]

        @pl.when(tile == 0)
        def _():
            ref[:, 7:8, :] = jnp.zeros((n, 1, COLS), F32)

        @pl.when(tile == TILES - 1)
        def _():
            ref[:, 24:25, :] = jnp.zeros((n, 1, COLS), F32)

    swap0 = swap_rows(x0, halo.at[0])

    flat_surf = surf.reshape(8 * FLUX * ROWS, 128)
    flat_bucket = bucket.reshape(TILES * FLUX * CAP, 128)

    def deliver(step, carry):
        dest = moved_tile(tile, step)
        for j in range(CAP):
            blk = rows[j, dest]
            start = (blk & 7) * (FLUX * ROWS) + (blk >> 3)
            flat_bucket[pl.ds(step * (FLUX * CAP) + j, FLUX, stride=CAP), :] = flat_surf[
                pl.ds(start, FLUX, stride=ROWS), :
            ]
        remote(bucket.at[step], arrived.at[step], send, recv.at[step >> 4], 1 - comp, dest).start()
        return carry

    lax.fori_loop(0, TILES, deliver, 0)

    basis_load.wait()
    lane = lax.broadcasted_iota(jnp.int32, (16, 128), 1)
    sub = lax.broadcasted_iota(jnp.int32, (16, 128), 0)
    rows_of = {}
    third = len(PAIRS) // 3
    for part in range(3):
        pairs = PAIRS[part * third : (part + 1) * third]

        def gram_step(n, acc, pairs=pairs):
            level = n >> 3
            at = pl.multiple_of((n & 7) * 128, 128)
            used = sorted({i for p in pairs for i in p})
            vals = {i: basis_v[i, level, :, pl.ds(at, 128)].astype(F32) for i in used}
            out = []
            for (i, j), a in zip(pairs, acc):
                p = vals[i] * vals[j]
                out.append(a + (p[:8] + p[8:]))
            return tuple(out)

        acc = lax.fori_loop(0, 64, gram_step, tuple(jnp.zeros((8, 128), F32) for _ in pairs))
        for p, a in zip(pairs, acc):
            rows_of[p] = jnp.sum(a, axis=0, keepdims=True)
    gram_here = jnp.zeros((16, 128), F32)
    for i in range(VECS):
        stack = jnp.concatenate(
            [rows_of[(min(i, j), max(i, j))] for j in range(VECS)] + [jnp.zeros((4, 128), F32)], axis=0
        )
        gram_here = jnp.where(lane == i, jnp.sum(stack, axis=1, keepdims=True), gram_here)
    g_mine[...] = gram_here

    kap_load.wait()
    vmix_load.wait()
    land_load.wait()
    maskf[...] = jnp.where(comp == 0, land_v[...].astype(F32), jnp.ones((ROWS, COLS), F32))
    for c in swap0:
        c.wait()
    clear_ends(x0)
    for l in range(LEV):
        x1[l, 8:24, :] = maskf[...] * (stencil(x0, l, kap[...]) + mixed(x0, vmix, l, LEV))
    swap1 = swap_rows(x1, halo.at[1])
    gram = sum_over_devices(comp, tile, g_mine, g_pair, g_wide, g_part, g_other, gsem)
    for c in swap1:
        c.wait()
    clear_ends(x1)
    for l in range(LEV):
        y[l] = maskf[...] * (stencil(x1, l, kap[...]) + mixed(x1, vmix, l, LEV))

    for c in table_loads:
        c.wait()
    slot = slots[...]
    src = slot >> 3
    a = (tile & 3) - (src & 3) & 3
    b = (tile >> 2 & 3) - (src >> 2 & 3) - a & 3
    c = (tile >> 4) - (src >> 4) - a & 3
    place = (a | b << 2 | c << 4) * CAP + (slot & 7)
    table = jnp.concatenate([place.astype(F32), weights[...], jnp.zeros((NB - 8, NB), F32)], axis=0).T
    at_lane = lax.broadcasted_iota(jnp.int32, (NB, TILES * CAP), 1).astype(F32)
    matrix = jnp.zeros((NB, TILES * CAP), F32)
    for k in range(4):
        matrix = matrix + jnp.where(at_lane == table[:, k : k + 1], table[:, 4 + k : 5 + k], 0.0)
    high = matrix.astype(BF16)
    low = (matrix - high.astype(F32)).astype(BF16)
    dot = functools.partial(jnp.dot, preferred_element_type=F32)
    sums = jnp.zeros((NB, FLUX * 128), F32)
    for g in range(GROUPS):
        wait_bytes(arrived.at[pl.ds(g * PER, PER)], recv.at[g])
        got = jnp.concatenate(
            [arrived[g * PER : (g + 1) * PER, i].reshape(PER * CAP, 128) for i in range(FLUX)], axis=1
        )
        got_high = got.astype(BF16)
        got_low = (got - got_high.astype(F32)).astype(BF16)
        cut = slice(g * PER * CAP, (g + 1) * PER * CAP)
        sums = sums + dot(high[:, cut], got_high) + dot(low[:, cut], got_high) + dot(high[:, cut], got_low)
    for i in range(FLUX):
        imp[i * NB : (i + 1) * NB, :] = sums[:, i * 128 : (i + 1) * 128]
    for i in range(FLUX):
        for j in range(8):
            piece = imp[pl.ds(i * NB + j, ROWS, stride=8), :]
            f[i, :, j * 128 : (j + 1) * 128] = piece
            fh[i, 8:24, j * 128 : (j + 1) * 128] = maskf[:, j * 128 : (j + 1) * 128] * piece
    swap2 = swap_rows(fh, halo.at[2])
    for c in swap2:
        c.wait()
    clear_ends(fh)
    for l in range(LEV):
        z = mixed(fh, vmix, l, FLUX)
        if l < FLUX:
            z = z + stencil(fh, l, kap[...]) + f[l]
        y[l] = y[l] + maskf[...] * z

    def dot_step(n, acc):
        level = n >> 3
        at = pl.multiple_of((n & 7) * 128, 128)
        x = y[level, :, pl.ds(at, 128)]
        out = [a + basis_v[i, level, :, pl.ds(at, 128)].astype(F32) * x for i, a in enumerate(acc[:VECS])]
        return tuple(out) + (acc[VECS] + x * x,)

    acc = lax.fori_loop(0, 64, dot_step, tuple(jnp.zeros((16, 128), F32) for _ in range(VECS + 1)))
    stack = jnp.concatenate([jnp.sum(a, axis=0, keepdims=True) for a in acc] + [jnp.zeros((3, 128), F32)], axis=0)
    col = jnp.sum(stack, axis=1, keepdims=True)
    e_mine[...] = jnp.sum(jnp.where(lane == sub, col, 0.0), axis=0, keepdims=True)
    dots = sum_over_devices(comp, tile, e_mine, e_pair, e_wide, e_part, e_other, esem)
    first = lax.broadcasted_iota(jnp.int32, (1, 128), 1)
    coef = jnp.where(first < VECS, dots * (1.0 / total), 0.0)
    coefs[...] = coef[0, :VECS]
    coef_col = jnp.sum(jnp.where(lane == sub, jnp.broadcast_to(coef, (16, 128)), 0.0), axis=1, keepdims=True)
    square = jnp.sum(jnp.where(first == VECS, dots, 0.0) - 2.0 * dots * coef, axis=1, keepdims=True)
    gc = jnp.sum(gram * coef, axis=1, keepdims=True)
    square = square + jnp.sum(gc * coef_col, axis=0, keepdims=True)
    scale = 1.0 / jnp.sqrt(jnp.maximum(square, 0.0) * (1.0 / total) + 1e-06)
    weigh = [jnp.broadcast_to(coef_col[i : i + 1] * scale, (16, 128)) for i in range(VECS)]
    scale = jnp.broadcast_to(scale, (16, 128))

    for l in range(LEV):

        def finish(n, carry):
            at = pl.multiple_of(n * 128, 128)
            w = scale * y[l, :, pl.ds(at, 128)]
            for i in range(VECS):
                w = w - weigh[i] * basis_v[i, l, :, pl.ds(at, 128)].astype(F32)
            direction[0, l, :, pl.ds(at, 128)] = w
            return carry

        lax.fori_loop(0, 8, finish, 0)
    wait_bytes(bucket, send)


def body(state, basis, kappa, vmix, land_mask, send_rows, recv_slots, recv_weights):
    vmem = pl.BlockSpec(memory_space=pltpu.VMEM)
    dma = pltpu.SemaphoreType.DMA
    pad = (LEV, 32, COLS)
    return pl.pallas_call(
        kernel,
        out_shape=(
            jax.ShapeDtypeStruct((1, LEV, ROWS, COLS), F32),
            jax.ShapeDtypeStruct((VECS,), F32),
        ),
        in_specs=[pl.BlockSpec(memory_space=pltpu.HBM)] * 8,
        out_specs=(vmem, vmem),
        scratch_shapes=[
            pltpu.VMEM((4, NB), jnp.int32),
            pltpu.VMEM((4, NB), F32),
            pltpu.SMEM((LEV, LEV), F32),
            pltpu.SMEM((CAP, TILES), jnp.int32),
            pltpu.VMEM(pad, F32),
            pltpu.VMEM(pad, F32),
            pltpu.VMEM((LEV, ROWS, COLS), F32),
            pltpu.VMEM((FLUX, 32, COLS), F32),
            pltpu.VMEM((FLUX, ROWS, COLS), F32),
            pltpu.VMEM((VECS, LEV, ROWS, COLS), BF16),
            pltpu.VMEM((ROWS, COLS), F32),
            pltpu.VMEM((ROWS, COLS), jnp.int32),
            pltpu.VMEM((ROWS, COLS), F32),
            pltpu.VMEM((8, FLUX, ROWS, 128), F32),
            pltpu.VMEM((TILES, FLUX, CAP, 128), F32),
            pltpu.VMEM((TILES, FLUX, CAP, 128), F32),
            pltpu.VMEM((FLUX * NB, 128), F32),
            pltpu.VMEM((16, 128), F32),
            pltpu.VMEM((16, 128), F32),
            pltpu.VMEM((TILES // 2, 16, 128), F32),
            pltpu.VMEM((16, 128), F32),
            pltpu.VMEM((16, 128), F32),
            pltpu.VMEM((1, 128), F32),
            pltpu.VMEM((1, 128), F32),
            pltpu.VMEM((TILES // 2, 1, 128), F32),
            pltpu.VMEM((1, 128), F32),
            pltpu.VMEM((1, 128), F32),
            dma((9,)),
            dma(()),
            dma((GROUPS,)),
            dma((3, 4)),
            dma((6,)),
            dma((6,)),
        ],
        compiler_params=pltpu.CompilerParams(
            collective_id=0, has_side_effects=True, vmem_limit_bytes=24 << 20
        ),
        name="interval",
    )(
        *(
            pltpu.with_memory_space_constraint(v, pltpu.HBM)
            for v in (
                state,
                basis,
                kappa,
                land_mask,
                jnp.swapaxes(recv_slots, 2, 3),
                jnp.swapaxes(recv_weights, 2, 3),
                vmix,
                jnp.swapaxes(send_rows, 2, 3),
            )
        )
    )


def solution(mesh):
    return jax.shard_map(
        body,
        mesh=mesh,
        in_specs=(
            P("comp", None, "tile", None),
            P(None, "comp", None, "tile", None),
            P("comp", "tile", None),
            P("comp", None, None),
            P("tile", None),
            P("comp", "tile", None, None),
            P("comp", "tile", None, None),
            P("comp", "tile", None, None),
        ),
        out_specs=(P("comp", None, "tile", None), P()),
        check_vma=False,
    )
```

```python
import functools

import jax
import jax.numpy as jnp
from jax import lax
from jax.experimental import pallas as pl
from jax.experimental.pallas import tpu as pltpu
from jax.sharding import PartitionSpec as P

FLUX = 4
VECS = 12
LEV = 8
ROWS = 16
COLS = 1024
TILES = 64
CAP = 8
NB = 128
GROUPS = 4
PER = TILES // GROUPS
MESH = pl.DeviceIdType.MESH
F32 = jnp.float32
BF16 = jnp.bfloat16
PAIRS = [(k, i, (i + k) % VECS) for k in range(VECS // 2 + 1) for i in range(VECS if k < VECS // 2 else VECS // 2)]
SEG = 16


def hops(k):
    return sum((0, 1, 2, 1)[(k >> s) & 3] for s in (0, 2, 4))


PEERS = [sorted((k for k in range(1, TILES) if k & 1 == c), key=lambda k: -hops(k)) for c in (0, 1)]


def offset_of(step):
    a, b, c = step & 3, (step >> 2) & 3, step >> 4
    return a, (a + b) & 3, (a + c) & 3


def moved_tile(tile, step):
    dx, dy, dz = offset_of(step)
    return ((tile & 3) + dx & 3) | (((tile >> 2 & 3) + dy & 3) << 2) | (((tile >> 4) + dz & 3) << 4)


def remote(src, dst, send, recv, comp, tile):
    return pltpu.make_async_remote_copy(
        src_ref=src, dst_ref=dst, send_sem=send, recv_sem=recv, device_id=(comp, tile), device_id_type=MESH
    )


def wait_bytes(ref, sem):
    pltpu.make_async_copy(ref, ref, sem).wait()


def sum_over_devices(comp, tile, mine, pair, wide, part, other, sems, meanwhile):
    first = remote(mine, pair, sems.at[0], sems.at[1], 1 - comp, tile)
    first.start()
    first.wait()
    chip = mine[...] + pair[...]
    part[...] = chip
    odd = tile & 1
    slot = tile >> 1

    for c in (0, 1):

        @pl.when(comp == c)
        def _():
            for k in PEERS[c]:
                remote(part, wide.at[slot], sems.at[2], sems.at[3], odd, tile ^ k).start()

    meanwhile()

    @pl.when(comp == odd)
    def _():
        wide[slot] = chip
        wait_bytes(wide.at[pl.ds(0, TILES // 2 - 1)], sems.at[3])

    @pl.when(comp != odd)
    def _():
        wait_bytes(wide.at[pl.ds(0, TILES // 2)], sems.at[3])

    half = wide[0]
    for s in range(1, TILES // 2):
        half = half + wide[s]
    for c in (0, 1):

        @pl.when(comp == c)
        def _():
            wait_bytes(wide.at[pl.ds(0, len(PEERS[c]))], sems.at[2])

    part[...] = half
    last = remote(part, other, sems.at[4], sems.at[5], 1 - comp, tile)
    last.start()
    last.wait()
    return half + other[...]


def stencil(ref, level, kap, row, count):
    x = ref[level, row : row + count, :]
    lap = (
        ref[level, row - 1 : row - 1 + count, :]
        + ref[level, row + 1 : row + 1 + count, :]
        + pltpu.roll(x, 1, 1)
        + pltpu.roll(x, COLS - 1, 1)
        - 4.0 * x
    )
    return x + kap * lap


def mixed(ref, vmix, level, terms, row, count):
    total = vmix[level, 0] * ref[0, row : row + count, :]
    for m in range(1, terms):
        total = total + vmix[level, m] * ref[m, row : row + count, :]
    return total


def kernel(
    state, basis, kappa, land, slots_hbm, weights_hbm, vmix_hbm, rows_hbm,
    x2, basis_v, result,
    slots, weights, vmix, rows, x0, x1, fh, f, kap, land_v, maskf, kap_far, land_far,
    surf, bucket, arrived, imp, edge_b, edge_out, edge_in, edge_k, edge_m, near,
    e_mine, e_pair, e_wide, e_part, e_other,
    load, send, recv, halo, esem,
):
    comp = lax.axis_index("comp")
    tile = lax.axis_index("tile")
    total = float(LEV * ROWS * COLS * TILES * 2)
    above = tile - 1 & TILES - 1
    below = tile + 1 & TILES - 1
    every = range(8)

    surf_loads = [
        pltpu.make_async_copy(
            state.at[0, pl.ds(0, FLUX), :, pl.ds(128 * j, 128)], surf.at[j], load.at[0]
        )
        for j in every
    ]
    for c in surf_loads:
        c.start()
    rows_load = pltpu.make_async_copy(rows_hbm.at[0, 0], rows, load.at[5])
    rows_load.start()
    x_load = pltpu.make_async_copy(state.at[0], x0.at[:, pl.ds(8, ROWS), :], load.at[1])
    x_load.start()
    kap_load = pltpu.make_async_copy(kappa.at[0], kap, load.at[2])
    kap_load.start()
    land_load = pltpu.make_async_copy(land, land_v, load.at[3])
    land_load.start()
    barrier = pltpu.get_barrier_semaphore()

    def greet(step, carry):
        pl.semaphore_signal(barrier, inc=1, device_id=(1 - comp, moved_tile(tile, step)), device_id_type=MESH)
        return carry

    lax.fori_loop(0, TILES, greet, 0)
    for t in (above, below):
        pl.semaphore_signal(barrier, inc=1, device_id=(comp, t), device_id_type=MESH)
    vmix_load = pltpu.make_async_copy(vmix_hbm.at[0], vmix, load.at[6])
    vmix_load.start()
    table_loads = [
        pltpu.make_async_copy(slots_hbm.at[0, 0], slots, load.at[7]),
        pltpu.make_async_copy(weights_hbm.at[0, 0], weights, load.at[8]),
    ]
    for c in table_loads:
        c.start()
    basis_load = pltpu.make_async_copy(basis.at[:, 0], basis_v, load.at[4])
    basis_load.start()
    for c in surf_loads:
        c.wait()
    rows_load.wait()
    x_load.wait()
    kap_load.wait()
    land_load.wait()
    pl.semaphore_wait(barrier, TILES + 2)

    swaps = [
        remote(x0.at[:, pl.ds(8, 2), :], x0.at[:, pl.ds(24, 2), :], halo.at[0], halo.at[1], comp, above),
        remote(x0.at[:, pl.ds(22, 2), :], x0.at[:, pl.ds(6, 2), :], halo.at[2], halo.at[3], comp, below),
        remote(kap.at[pl.ds(0, 1)], kap_far.at[1], halo.at[4], halo.at[5], comp, above),
        remote(kap.at[pl.ds(15, 1)], kap_far.at[0], halo.at[6], halo.at[7], comp, below),
        remote(land_v.at[pl.ds(0, 1)], land_far.at[1], halo.at[8], halo.at[9], comp, above),
        remote(land_v.at[pl.ds(15, 1)], land_far.at[0], halo.at[10], halo.at[11], comp, below),
    ]
    for c in swaps:
        c.start()

    flat_surf = surf.reshape(8 * FLUX * ROWS, 128)
    flat_bucket = bucket.reshape(TILES * FLUX * CAP, 128)

    def deliver(step, carry):
        dest = moved_tile(tile, step)
        for j in range(CAP):
            blk = rows[j, dest]
            start = (blk & 7) * (FLUX * ROWS) + (blk >> 3)
            flat_bucket[pl.ds(step * (FLUX * CAP) + j, FLUX, stride=CAP), :] = flat_surf[
                pl.ds(start, FLUX, stride=ROWS), :
            ]
        remote(bucket.at[step], arrived.at[step], send, recv.at[step >> 4], 1 - comp, dest).start()
        return carry

    lax.fori_loop(0, TILES, deliver, 0)

    vmix_load.wait()
    maskf[...] = jnp.where(comp == 0, land_v[...].astype(F32), jnp.ones((ROWS, COLS), F32))
    for c in swaps:
        c.wait()

    @pl.when(tile == 0)
    def _():
        x0[:, 6:8, :] = jnp.zeros((LEV, 2, COLS), F32)

    @pl.when(tile == TILES - 1)
    def _():
        x0[:, 24:26, :] = jnp.zeros((LEV, 2, COLS), F32)

    for l in range(LEV):
        x1[l, 8:24, :] = maskf[...] * (stencil(x0, l, kap[...], 8, ROWS) + mixed(x0, vmix, l, LEV, 8, ROWS))
    for end, row, last in ((0, 7, 0), (1, 24, TILES - 1)):
        far = jnp.where(comp == 0, land_far[end].astype(F32), jnp.ones((1, COLS), F32))
        far = jnp.where(tile == last, jnp.zeros((1, COLS), F32), far)
        for l in range(LEV):
            x1[l, row : row + 1, :] = far * (
                stencil(x0, l, kap_far[end], row, 1) + mixed(x0, vmix, l, LEV, row, 1)
            )
    for l in range(LEV):
        x2[l] = maskf[...] * (stencil(x1, l, kap[...], 8, ROWS) + mixed(x1, vmix, l, LEV, 8, ROWS))

    for j in every:
        cut = slice(j * 128, (j + 1) * 128)
        for end, row in ((0, 0), (1, 15)):
            m = maskf[row : row + 1, cut]
            edge_m[end, j : j + 1] = m
            edge_k[end, j : j + 1] = m * kap[row : row + 1, cut]
    fh[:, 7:8, :] = jnp.zeros((FLUX, 1, COLS), F32)
    fh[:, 24:25, :] = jnp.zeros((FLUX, 1, COLS), F32)

    for c in table_loads:
        c.wait()
    slot = slots[...]
    src = slot >> 3
    a = (tile & 3) - (src & 3) & 3
    b = (tile >> 2 & 3) - (src >> 2 & 3) - a & 3
    c = (tile >> 4) - (src >> 4) - a & 3
    place = (a | b << 2 | c << 4) * CAP + (slot & 7)
    table = jnp.concatenate([place.astype(F32), weights[...], jnp.zeros((NB - 8, NB), F32)], axis=0).T
    at_lane = lax.broadcasted_iota(jnp.int32, (NB, TILES * CAP), 1).astype(F32)
    matrix = jnp.zeros((NB, TILES * CAP), F32)
    for k in range(4):
        matrix = matrix + jnp.where(at_lane == table[:, k : k + 1], table[:, 4 + k : 5 + k], 0.0)
    ends = jnp.concatenate([matrix[:8], matrix[-8:]], axis=0)

    def halves(v):
        high = v.astype(BF16)
        return high, (v - high.astype(F32)).astype(BF16)

    high, low = halves(matrix)
    ends_high, ends_low = halves(ends)

    basis_load.wait()
    lane = lax.broadcasted_iota(jnp.int32, (SEG, 128), 1)
    sub = lax.broadcasted_iota(jnp.int32, (SEG, 128), 0)
    rows_of = {}
    third = len(PAIRS) // 3
    for part in range(3):
        pairs = PAIRS[part * third : (part + 1) * third]

        def gram_step(n, acc, pairs=pairs):
            level = n >> 3
            at = pl.multiple_of((n & 7) * 128, 128)
            used = sorted({i for p in pairs for i in p[1:]})
            vals = {i: basis_v[i, level, :, pl.ds(at, 128)].astype(F32) for i in used}
            out = []
            for (_, i, j), a in zip(pairs, acc):
                p = vals[i] * vals[j]
                out.append(a + (p[:8] + p[8:]))
            return tuple(out)

        acc = lax.fori_loop(0, 64, gram_step, tuple(jnp.zeros((8, 128), F32) for _ in pairs))
        for (k, i, _), a in zip(pairs, acc):
            rows_of[k, i] = jnp.sum(a, axis=0, keepdims=True)
    empty = jnp.zeros((1, 128), F32)

    def to_lanes(rows_, k):
        stack = jnp.concatenate(rows_ + [empty] * (SEG - len(rows_)), axis=0)
        return jnp.where(lane == sub + SEG * k, jnp.sum(stack, axis=1, keepdims=True), 0.0)

    gram = jnp.zeros((SEG, 128), F32)
    for k in range(VECS // 2 + 1):
        gram = gram + to_lanes([rows_of[k, i] for i in range(VECS) if (k, i) in rows_of], k)

    def edge_step(i, carry):
        for l in range(FLUX):
            for j in every:
                v = basis_v[i, l, :, j * 128 : (j + 1) * 128].astype(F32)
                edge_b[i, l, 0, j : j + 1] = v[:1]
                edge_b[i, l, 1, j : j + 1] = v[15:]
        return carry

    lax.fori_loop(0, VECS, edge_step, 0)

    dot = functools.partial(jnp.dot, preferred_element_type=F32)

    def group(g):
        wait_bytes(arrived.at[pl.ds(g * PER, PER)], recv.at[g])
        got = jnp.concatenate(
            [arrived[g * PER : (g + 1) * PER, i].reshape(PER * CAP, 128) for i in range(FLUX)], axis=1
        )
        return slice(g * PER * CAP, (g + 1) * PER * CAP), *halves(got)

    def times(high, low, cut, got_high, got_low):
        return dot(high[:, cut], got_high) + dot(low[:, cut], got_high) + dot(high[:, cut], got_low)

    sums = jnp.zeros((NB, FLUX * 128), F32)
    for g in range(GROUPS - 1):
        sums = sums + times(high, low, *group(g))
    tail = group(GROUPS - 1)
    border = jnp.concatenate([sums[:8], sums[-8:]], axis=0) + times(ends_high, ends_low, *tail)
    for end in (0, 1):
        for i in range(FLUX):
            edge_out[end, i] = edge_m[end] * border[end * 8 : end * 8 + 8, i * 128 : (i + 1) * 128]
    edges = [
        remote(edge_out.at[0], edge_in.at[1], halo.at[12], halo.at[13], comp, above),
        remote(edge_out.at[1], edge_in.at[0], halo.at[14], halo.at[15], comp, below),
    ]
    for c in edges:
        c.start()
    sums = sums + times(high, low, *tail)
    for i in range(FLUX):
        imp[i * NB : (i + 1) * NB, :] = sums[:, i * 128 : (i + 1) * 128]
    for i in range(FLUX):
        for j in every:
            cut = slice(j * 128, (j + 1) * 128)
            piece = imp[pl.ds(i * NB + j, ROWS, stride=8), :]
            f[i, :, cut] = piece
            fh[i, 8:24, cut] = maskf[:, cut] * piece
    for l in range(LEV):
        z = mixed(fh, vmix, l, FLUX, 8, ROWS)
        if l < FLUX:
            z = z + stencil(fh, l, kap[...], 8, ROWS) + f[l]
        x2[l] = x2[l] + maskf[...] * z

    def dot_step(n, acc):
        level = n >> 2
        for half in (0, 1):
            at = pl.multiple_of((n & 3) * 256 + half * 128, 128)
            x = x2[level, :, pl.ds(at, 128)]
            out = [a + basis_v[i, level, :, pl.ds(at, 128)].astype(F32) * x for i, a in enumerate(acc[:VECS])]
            acc = tuple(out) + (acc[VECS] + x * x,)
        return acc

    acc = lax.fori_loop(0, 32, dot_step, tuple(jnp.zeros((16, 128), F32) for _ in range(VECS + 1)))
    acc = [a[:8] + a[8:] for a in acc]
    for l in range(FLUX):
        for end, row in ((0, 0), (1, 15)):
            for j in every:
                near[l, end, j : j + 1] = x2[l, row : row + 1, j * 128 : (j + 1) * 128]
    for c in edges:
        c.wait()
    extra = {}
    for end, last in ((0, 0), (1, TILES - 1)):
        factor = jnp.where(tile == last, jnp.zeros((8, 128), F32), edge_k[end])
        for l in range(FLUX):
            add = factor * edge_in[end, l]
            extra[l, end] = add
            for i in range(VECS):
                acc[i] = acc[i] + edge_b[i, l, end] * add
            acc[VECS] = acc[VECS] + add * (2.0 * near[l, end] + add)
    sums_of = [jnp.sum(a, axis=0, keepdims=True) for a in acc]
    e_mine[...] = jnp.sum(gram + to_lanes(sums_of, 7), axis=0, keepdims=True)

    def add_edges():
        for (l, end), add in extra.items():
            row = 15 * end
            full = near[l, end] + add
            for j in every:
                x2[l, row : row + 1, j * 128 : (j + 1) * 128] = full[j : j + 1]

    dots = sum_over_devices(comp, tile, e_mine, e_pair, e_wide, e_part, e_other, esem, add_edges)

    one = lax.broadcasted_iota(jnp.int32, (1, 128), 1)
    seg, pos = one >> 4, one & 15
    vals = jnp.where((seg == 7) & (pos < VECS), dots * (1.0 / total), 0.0)
    coef = pltpu.roll(vals, SEG, 1)
    twice = coef + pltpu.roll(coef, VECS, 1)
    left = jnp.zeros((1, 128), F32)
    right = jnp.zeros((1, 128), F32)
    for k in range(VECS // 2 + 1):
        left = jnp.where(seg == k, pltpu.roll(coef, SEG * k, 1) if k else coef, left)
        right = jnp.where(seg == k, pltpu.roll(twice, (SEG - 1) * k, 1) if k else twice, right)
    factor = jnp.where(seg == 0, 1.0, 2.0)
    products = jnp.where((seg < 7) & (pos < VECS), factor * dots * left * right, 0.0)
    square = jnp.where((seg == 7) & (pos == VECS), dots, 0.0) - 2.0 * dots * vals + products
    square = jnp.sum(square, axis=1, keepdims=True)
    scale = 1.0 / jnp.sqrt(jnp.maximum(square, 0.0) * (1.0 / total) + 1e-06)
    line = jnp.where(one == VECS, 1.0, coef)
    column = jnp.sum(jnp.where(lane == sub, jnp.broadcast_to(line, (SEG, 128)), 0.0), axis=1, keepdims=True)
    result[0:SEG] = jnp.broadcast_to(column * scale, (SEG, 128))
    result[SEG : SEG + 1] = coef
    wait_bytes(bucket, send)


def finish(x2, basis_v, result, direction, coefs, out, store):
    coefs[...] = result[SEG, :VECS]
    for l in range(LEV):

        def part(n, carry):
            at = pl.multiple_of(n * 128, 128)
            w = result[VECS : VECS + 1] * x2[l, :, pl.ds(at, 128)]
            for i in range(VECS):
                w = w - result[i : i + 1] * basis_v[i, l, :, pl.ds(at, 128)].astype(F32)
            out[l, :, pl.ds(at, 128)] = w
            return carry

        lax.fori_loop(0, 8, part, 0)
        pltpu.make_async_copy(out.at[l], direction.at[0, l], store).start()
    wait_bytes(out, store)


def body(state, basis, kappa, vmix, land_mask, send_rows, recv_slots, recv_weights):
    vmem = pl.BlockSpec(memory_space=pltpu.VMEM)
    dma = pltpu.SemaphoreType.DMA
    pad = (LEV, 32, COLS)
    band = (ROWS, COLS)
    ints = jnp.int32
    scratch = [((4, NB), ints), ((4, NB), F32), None, None, (pad, F32), (pad, F32)]
    scratch += [((FLUX, 32, COLS), F32), ((FLUX, ROWS, COLS), F32), (band, F32), (band, ints), (band, F32)]
    scratch += [((2, 1, COLS), F32), ((2, 1, COLS), ints), ((8, FLUX, ROWS, 128), F32)]
    scratch += [((TILES, FLUX, CAP, 128), F32)] * 2 + [((FLUX * NB, 128), F32)]
    scratch += [((VECS, FLUX, 2, 8, 128), F32)] + [((2, FLUX, 8, 128), F32)] * 2 + [((2, 8, 128), F32)] * 2
    scratch += [((FLUX, 2, 8, 128), F32)]
    scratch += [((1, 128), F32)] * 2 + [((TILES // 2, 1, 128), F32)] + [((1, 128), F32)] * 2
    scratch = [pltpu.VMEM(*v) if v else None for v in scratch]
    scratch[2] = pltpu.SMEM((LEV, LEV), F32)
    scratch[3] = pltpu.SMEM((CAP, TILES), ints)
    x2, basis_v, result = pl.pallas_call(
        kernel,
        out_shape=(
            jax.ShapeDtypeStruct((LEV, ROWS, COLS), F32),
            jax.ShapeDtypeStruct((VECS, LEV, ROWS, COLS), BF16),
            jax.ShapeDtypeStruct((SEG + 8, 128), F32),
        ),
        in_specs=[pl.BlockSpec(memory_space=pltpu.HBM)] * 8,
        out_specs=(vmem,) * 3,
        scratch_shapes=scratch + [dma((9,)), dma(()), dma((GROUPS,)), dma((16,)), dma((6,))],
        compiler_params=pltpu.CompilerParams(
            collective_id=0, has_side_effects=True, vmem_limit_bytes=24 << 20
        ),
        name="interval",
    )(
        *(
            pltpu.with_memory_space_constraint(v, pltpu.HBM)
            for v in (
                state,
                basis,
                kappa,
                land_mask,
                jnp.swapaxes(recv_slots, 2, 3),
                jnp.swapaxes(recv_weights, 2, 3),
                vmix,
                jnp.swapaxes(send_rows, 2, 3),
            )
        )
    )
    return pl.pallas_call(
        finish,
        out_shape=(
            jax.ShapeDtypeStruct((1, LEV, ROWS, COLS), F32),
            jax.ShapeDtypeStruct((VECS,), F32),
        ),
        in_specs=[vmem] * 3,
        out_specs=(pl.BlockSpec(memory_space=pl.ANY), vmem),
        scratch_shapes=[pltpu.VMEM((LEV, ROWS, COLS), F32), dma(())],
        compiler_params=pltpu.CompilerParams(vmem_limit_bytes=16 << 20),
        name="finish",
    )(x2, basis_v, result)


def solution(mesh):
    return jax.shard_map(
        body,
        mesh=mesh,
        in_specs=(
            P("comp", None, "tile", None),
            P(None, "comp", None, "tile", None),
            P("comp", "tile", None),
            P("comp", None, None),
            P("tile", None),
            P("comp", "tile", None, None),
            P("comp", "tile", None, None),
            P("comp", "tile", None, None),
        ),
        out_specs=(P("comp", None, "tile", None), P()),
        check_vma=False,
    )
```

```python
import functools

import jax
import jax.numpy as jnp
from jax import lax
from jax.experimental import pallas as pl
from jax.experimental.pallas import tpu as pltpu
from jax.sharding import PartitionSpec as P

FLUX = 4
VECS = 12
LEV = 8
ROWS = 16
COLS = 1024
TILES = 64
CAP = 8
NB = 128
GROUPS = 4
PER = TILES // GROUPS
MESH = pl.DeviceIdType.MESH
F32 = jnp.float32
BF16 = jnp.bfloat16
SEG = 16


def hops(k):
    return sum((0, 1, 2, 1)[(k >> s) & 3] for s in (0, 2, 4))


FAR_FIRST = sorted(range(TILES), key=lambda k: -hops(k))


PEERS = [sorted((k for k in range(1, TILES) if k & 1 == c), key=lambda k: -hops(k)) for c in (0, 1)]


def offset_of(step):
    a, b, c = step & 3, (step >> 2) & 3, step >> 4
    return a, (b - a) & 3, (a + c) & 3


def moved_tile(tile, step):
    dx, dy, dz = offset_of(step)
    return ((tile & 3) + dx & 3) | (((tile >> 2 & 3) + dy & 3) << 2) | (((tile >> 4) + dz & 3) << 4)


def remote(src, dst, send, recv, comp, tile):
    return pltpu.make_async_remote_copy(
        src_ref=src, dst_ref=dst, send_sem=send, recv_sem=recv, device_id=(comp, tile), device_id_type=MESH
    )


def wait_bytes(ref, sem):
    pltpu.make_async_copy(ref, ref, sem).wait()


def sum_over_devices(comp, tile, mine, pair, wide, part, other, sems, meanwhile):
    first = remote(mine, pair, sems.at[0], sems.at[1], 1 - comp, tile)
    first.start()
    first.wait()
    chip = mine[...] + pair[...]
    part[...] = chip
    odd = tile & 1
    slot = tile >> 1

    for c in (0, 1):

        @pl.when(comp == c)
        def _():
            for k in PEERS[c]:
                remote(part, wide.at[slot], sems.at[2], sems.at[3], odd, tile ^ k).start()

    meanwhile()

    @pl.when(comp == odd)
    def _():
        wide[slot] = chip
        wait_bytes(wide.at[pl.ds(0, TILES // 2 - 1)], sems.at[3])

    @pl.when(comp != odd)
    def _():
        wait_bytes(wide.at[pl.ds(0, TILES // 2)], sems.at[3])

    half = wide[0]
    for s in range(1, TILES // 2):
        half = half + wide[s]
    for c in (0, 1):

        @pl.when(comp == c)
        def _():
            wait_bytes(wide.at[pl.ds(0, len(PEERS[c]))], sems.at[2])

    part[...] = half
    last = remote(part, other, sems.at[4], sems.at[5], 1 - comp, tile)
    last.start()
    last.wait()
    return half + other[...]


def stencil(ref, level, kap):
    x = ref[level, 8:24, :]
    lap = (
        ref[level, 7:23, :]
        + ref[level, 9:25, :]
        + pltpu.roll(x, 1, 1)
        + pltpu.roll(x, COLS - 1, 1)
        - 4.0 * x
    )
    return x + kap * lap


def mixed(ref, vmix, level, terms):
    total = vmix[level, 0] * ref[0, 8:24, :]
    for m in range(1, terms):
        total = total + vmix[level, m] * ref[m, 8:24, :]
    return total


def kernel(
    state, basis, kappa, land, slots_hbm, weights_hbm, vmix_hbm, rows_hbm,
    x2, basis_v, result,
    slots, weights, vmix, rows, x0, x1, fh, f, kap, land_v, maskf, gram_v, edge_x,
    surf, bucket, arrived, imp, edge_b, edge_out, edge_in, edge_k, edge_m, near,
    e_mine, e_pair, e_wide, e_part, e_other,
    load, send, recv, halo, esem,
):
    comp = lax.axis_index("comp")
    tile = lax.axis_index("tile")
    total = float(LEV * ROWS * COLS * TILES * 2)
    above = tile - 1 & TILES - 1
    below = tile + 1 & TILES - 1
    every = range(8)

    barrier = pltpu.get_barrier_semaphore()

    def greet(ks):
        for k in ks:
            pl.semaphore_signal(barrier, inc=1, device_id=(1 - comp, tile ^ k), device_id_type=MESH)

    greet(FAR_FIRST[:32])
    surf_loads = [
        pltpu.make_async_copy(
            state.at[0, pl.ds(0, FLUX), :, pl.ds(128 * j, 128)], surf.at[j], load.at[0]
        )
        for j in every
    ]
    rows_load = pltpu.make_async_copy(rows_hbm.at[0, 0], rows, load.at[5])
    x_load = pltpu.make_async_copy(state.at[0], x0.at[:, pl.ds(8, ROWS), :], load.at[1])
    for c in [rows_load, x_load, *surf_loads]:
        c.start()
    greet(FAR_FIRST[32:])
    for t in (above, below):
        pl.semaphore_signal(barrier, inc=1, device_id=(comp, t), device_id_type=MESH)
    kap_load = pltpu.make_async_copy(kappa.at[0], kap, load.at[2])
    kap_load.start()
    land_load = pltpu.make_async_copy(land, land_v, load.at[3])
    land_load.start()
    vmix_load = pltpu.make_async_copy(vmix_hbm.at[0], vmix, load.at[6])
    vmix_load.start()
    table_loads = [
        pltpu.make_async_copy(slots_hbm.at[0, 0], slots, load.at[7]),
        pltpu.make_async_copy(weights_hbm.at[0, 0], weights, load.at[8]),
    ]
    for c in table_loads:
        c.start()
    basis_load = pltpu.make_async_copy(basis.at[:, 0], basis_v, load.at[4])
    basis_load.start()
    rows_load.wait()
    x_load.wait()
    for c in surf_loads:
        c.wait()
    pl.semaphore_wait(barrier, TILES + 2)

    def swap_rows(ref, sems):
        pair = [
            remote(ref.at[:, pl.ds(8, 1), :], ref.at[:, pl.ds(24, 1), :], sems.at[0], sems.at[1], comp, above),
            remote(ref.at[:, pl.ds(23, 1), :], ref.at[:, pl.ds(7, 1), :], sems.at[2], sems.at[3], comp, below),
        ]
        for c in pair:
            c.start()
        return pair

    def clear_ends(ref):
        n = ref.shape[0]

        @pl.when(tile == 0)
        def _():
            ref[:, 7:8, :] = jnp.zeros((n, 1, COLS), F32)

        @pl.when(tile == TILES - 1)
        def _():
            ref[:, 24:25, :] = jnp.zeros((n, 1, COLS), F32)

    swap = swap_rows(x0, halo.at[0])

    flat_surf = surf.reshape(8 * FLUX * ROWS, 128)
    flat_bucket = bucket.reshape(TILES * FLUX * CAP, 128)

    def deliver(step, carry):
        dest = moved_tile(tile, step)
        for j in range(CAP):
            blk = rows[j, dest]
            start = (blk & 7) * (FLUX * ROWS) + (blk >> 3)
            flat_bucket[pl.ds(step * (FLUX * CAP) + j, FLUX, stride=CAP), :] = flat_surf[
                pl.ds(start, FLUX, stride=ROWS), :
            ]
        remote(bucket.at[step], arrived.at[step], send, recv.at[step >> 4], 1 - comp, dest).start()
        return carry

    lax.fori_loop(0, TILES // 2, deliver, 0)

    vmix_load.wait()
    kap_load.wait()
    land_load.wait()
    maskf[...] = jnp.where(comp == 0, land_v[...].astype(F32), jnp.ones((ROWS, COLS), F32))
    for c in swap:
        c.wait()
    clear_ends(x0)
    for l in range(LEV):
        x1[l, 8:24, :] = maskf[...] * (stencil(x0, l, kap[...]) + mixed(x0, vmix, l, LEV))
    deep = x1.at[pl.ds(FLUX, LEV - FLUX)]
    for row in (7, 24):
        x1[0:FLUX, row : row + 1, :] = jnp.zeros((FLUX, 1, COLS), F32)
        fh[:, row : row + 1, :] = jnp.zeros((FLUX, 1, COLS), F32)
    swap = swap_rows(deep, halo.at[1])
    lax.fori_loop(TILES // 2, TILES, deliver, 0)

    for j in every:
        cut = slice(j * 128, (j + 1) * 128)
        for end, row in ((0, 0), (1, 15)):
            m = maskf[row : row + 1, cut]
            edge_m[end, j : j + 1] = m
            edge_k[end, j : j + 1] = m * kap[row : row + 1, cut]
            for l in range(FLUX):
                edge_x[end, l, j : j + 1] = x1[l, 8 + row : 9 + row, cut]
    for l in range(FLUX):
        x2[l] = maskf[...] * (stencil(x1, l, kap[...]) + mixed(x1, vmix, l, LEV))

    for c in table_loads:
        c.wait()
    slot = slots[...]
    src = slot >> 3
    a = (tile & 3) - (src & 3) & 3
    b = (tile >> 2 & 3) - (src >> 2 & 3) + a & 3
    c = (tile >> 4) - (src >> 4) - a & 3
    place = (a | b << 2 | c << 4) * CAP + (slot & 7)
    table = jnp.concatenate([place.astype(F32), weights[...], jnp.zeros((NB - 8, NB), F32)], axis=0).T
    at_lane = lax.broadcasted_iota(jnp.int32, (NB, TILES * CAP), 1).astype(F32)
    matrix = jnp.zeros((NB, TILES * CAP), F32)
    for k in range(4):
        matrix = matrix + jnp.where(at_lane == table[:, k : k + 1], table[:, 4 + k : 5 + k], 0.0)
    ends = jnp.concatenate([matrix[:8], matrix[-8:]], axis=0)

    def halves(v):
        high = v.astype(BF16)
        return high, (v - high.astype(F32)).astype(BF16)

    high, low = halves(matrix)
    ends_high, ends_low = halves(ends)

    basis_load.wait()
    lane = lax.broadcasted_iota(jnp.int32, (SEG, 128), 1)
    sub = lax.broadcasted_iota(jnp.int32, (SEG, 128), 0)

    def gram_step(n, acc):
        level = n >> 2
        at = pl.multiple_of((n & 3) * 256, 256)
        x = jnp.concatenate([basis_v[i, level, :, pl.ds(at, 256)] for i in range(VECS)], axis=0)
        gram_v[...] += lax.dot_general(x, x, (((1,), (1,)), ((), ())), preferred_element_type=F32)
        return acc

    span = VECS * ROWS
    gram_v[...] = jnp.zeros((span, span), F32)
    lax.fori_loop(0, 32, gram_step, 0)
    row_of = lax.broadcasted_iota(jnp.int32, (ROWS, span), 0)
    col_of = lax.broadcasted_iota(jnp.int32, (ROWS, span), 1)
    diagonal = row_of == (col_of & ROWS - 1)
    picked = [
        jnp.sum(jnp.where(diagonal, gram_v[i * ROWS : (i + 1) * ROWS, :], 0.0), axis=0, keepdims=True)
        for i in range(VECS)
    ]
    picked = jnp.concatenate(picked + [jnp.zeros((SEG - VECS, span), F32)], axis=0)
    gather = lax.broadcasted_iota(jnp.int32, (span, 128), 0) >> 4 == lax.broadcasted_iota(jnp.int32, (span, 128), 1)
    square = jnp.dot(picked, gather.astype(F32), precision=lax.Precision.HIGHEST, preferred_element_type=F32)
    empty = jnp.zeros((1, 128), F32)

    def to_lanes(rows_, k):
        stack = jnp.concatenate(rows_ + [empty] * (SEG - len(rows_)), axis=0)
        return jnp.where(lane == sub + SEG * k, jnp.sum(stack, axis=1, keepdims=True), 0.0)

    gram = jnp.zeros((SEG, 128), F32)
    for k in range(VECS // 2 + 1):
        other = jnp.where(sub + k >= VECS, sub + k - VECS, sub + k)
        own = sub < (VECS if k < VECS // 2 else VECS // 2)
        col = jnp.sum(jnp.where((lane == other) & own, square, 0.0), axis=1, keepdims=True)
        gram = gram + jnp.where(lane == sub + SEG * k, col, 0.0)

    for c in swap:
        c.wait()
    clear_ends(deep)
    for l in range(FLUX, LEV):
        x2[l] = maskf[...] * (stencil(x1, l, kap[...]) + mixed(x1, vmix, l, LEV))

    def edge_step(i, carry):
        for l in range(FLUX):
            for j in every:
                v = basis_v[i, l, :, j * 128 : (j + 1) * 128].astype(F32)
                edge_b[i, l, 0, j : j + 1] = v[:1]
                edge_b[i, l, 1, j : j + 1] = v[15:]
        return carry

    lax.fori_loop(0, VECS, edge_step, 0)

    dot = functools.partial(jnp.dot, preferred_element_type=F32)

    def group(g):
        wait_bytes(arrived.at[pl.ds(g * PER, PER)], recv.at[g])
        got = jnp.concatenate(
            [arrived[g * PER : (g + 1) * PER, i].reshape(PER * CAP, 128) for i in range(FLUX)], axis=1
        )
        return slice(g * PER * CAP, (g + 1) * PER * CAP), *halves(got)

    def times(high, low, cut, got_high, got_low):
        return dot(high[:, cut], got_high) + dot(low[:, cut], got_high) + dot(high[:, cut], got_low)

    sums = jnp.zeros((NB, FLUX * 128), F32)
    for g in range(GROUPS - 1):
        sums = sums + times(high, low, *group(g))
    tail = group(GROUPS - 1)
    border = jnp.concatenate([sums[:8], sums[-8:]], axis=0) + times(ends_high, ends_low, *tail)
    for end in (0, 1):
        for i in range(FLUX):
            edge_out[end, i] = edge_x[end, i] + edge_m[end] * border[end * 8 : end * 8 + 8, i * 128 : (i + 1) * 128]
    edges = [
        remote(edge_out.at[0], edge_in.at[1], halo.at[2, 0], halo.at[2, 1], comp, above),
        remote(edge_out.at[1], edge_in.at[0], halo.at[2, 2], halo.at[2, 3], comp, below),
    ]
    for c in edges:
        c.start()
    sums = sums + times(high, low, *tail)
    for i in range(FLUX):
        imp[i * NB : (i + 1) * NB, :] = sums[:, i * 128 : (i + 1) * 128]
    for i in range(FLUX):
        for j in every:
            cut = slice(j * 128, (j + 1) * 128)
            piece = imp[pl.ds(i * NB + j, ROWS, stride=8), :]
            f[i, :, cut] = piece
            fh[i, 8:24, cut] = maskf[:, cut] * piece
    for l in range(LEV):
        z = mixed(fh, vmix, l, FLUX)
        if l < FLUX:
            z = z + stencil(fh, l, kap[...]) + f[l]
        x2[l] = x2[l] + maskf[...] * z

    def dot_step(n, acc):
        level = n >> 2
        for half in (0, 1):
            at = pl.multiple_of((n & 3) * 256 + half * 128, 128)
            x = x2[level, :, pl.ds(at, 128)]
            out = [a + basis_v[i, level, :, pl.ds(at, 128)].astype(F32) * x for i, a in enumerate(acc[:VECS])]
            acc = tuple(out) + (acc[VECS] + x * x,)
        return acc

    acc = lax.fori_loop(0, 32, dot_step, tuple(jnp.zeros((16, 128), F32) for _ in range(VECS + 1)))
    acc = [a[:8] + a[8:] for a in acc]
    for l in range(FLUX):
        for end, row in ((0, 0), (1, 15)):
            for j in every:
                near[l, end, j : j + 1] = x2[l, row : row + 1, j * 128 : (j + 1) * 128]
    for c in edges:
        c.wait()
    extra = {}
    for end, last in ((0, 0), (1, TILES - 1)):
        factor = jnp.where(tile == last, jnp.zeros((8, 128), F32), edge_k[end])
        for l in range(FLUX):
            add = factor * edge_in[end, l]
            extra[l, end] = add
            for i in range(VECS):
                acc[i] = acc[i] + edge_b[i, l, end] * add
            acc[VECS] = acc[VECS] + add * (2.0 * near[l, end] + add)
    sums_of = [jnp.sum(a, axis=0, keepdims=True) for a in acc]
    e_mine[...] = jnp.sum(gram + to_lanes(sums_of, 7), axis=0, keepdims=True)

    def add_edges():
        for (l, end), add in extra.items():
            row = 15 * end
            full = near[l, end] + add
            for j in every:
                x2[l, row : row + 1, j * 128 : (j + 1) * 128] = full[j : j + 1]

    dots = sum_over_devices(comp, tile, e_mine, e_pair, e_wide, e_part, e_other, esem, add_edges)

    one = lax.broadcasted_iota(jnp.int32, (1, 128), 1)
    seg, pos = one >> 4, one & 15
    vals = jnp.where((seg == 7) & (pos < VECS), dots * (1.0 / total), 0.0)
    coef = pltpu.roll(vals, SEG, 1)
    twice = coef + pltpu.roll(coef, VECS, 1)
    left = jnp.zeros((1, 128), F32)
    right = jnp.zeros((1, 128), F32)
    for k in range(VECS // 2 + 1):
        left = jnp.where(seg == k, pltpu.roll(coef, SEG * k, 1) if k else coef, left)
        right = jnp.where(seg == k, pltpu.roll(twice, (SEG - 1) * k, 1) if k else twice, right)
    factor = jnp.where(seg == 0, 1.0, 2.0)
    products = jnp.where((seg < 7) & (pos < VECS), factor * dots * left * right, 0.0)
    square = jnp.where((seg == 7) & (pos == VECS), dots, 0.0) - 2.0 * dots * vals + products
    square = jnp.sum(square, axis=1, keepdims=True)
    scale = 1.0 / jnp.sqrt(jnp.maximum(square, 0.0) * (1.0 / total) + 1e-06)
    line = jnp.where(one == VECS, 1.0, coef)
    column = jnp.sum(jnp.where(lane == sub, jnp.broadcast_to(line, (SEG, 128)), 0.0), axis=1, keepdims=True)
    result[0:SEG] = jnp.broadcast_to(column * scale, (SEG, 128))
    result[SEG : SEG + 1] = coef
    wait_bytes(bucket, send)


def finish(x2, basis_v, result, direction, coefs, out, line, store, small):
    line[...] = result[SEG, :VECS]
    first = pltpu.make_async_copy(line, coefs, small)
    first.start()
    weigh = [jnp.broadcast_to(result[i : i + 1], (ROWS, 128)) for i in range(VECS + 1)]
    for l in range(LEV):

        def part(n, carry):
            for half in (0, 1):
                at = pl.multiple_of(n * 256 + half * 128, 128)
                w = weigh[VECS] * x2[l, :, pl.ds(at, 128)]
                for i in range(VECS):
                    w = w - weigh[i] * basis_v[i, l, :, pl.ds(at, 128)].astype(F32)
                out[l, :, pl.ds(at, 128)] = w
            return carry

        lax.fori_loop(0, 4, part, 0)
        pltpu.make_async_copy(out.at[l], direction.at[0, l], store).start()
    first.wait()
    wait_bytes(out, store)


def body(state, basis, kappa, vmix, land_mask, send_rows, recv_slots, recv_weights):
    vmem = pl.BlockSpec(memory_space=pltpu.VMEM)
    dma = pltpu.SemaphoreType.DMA
    pad = (LEV, 32, COLS)
    band = (ROWS, COLS)
    ints = jnp.int32
    scratch = [((4, NB), ints), ((4, NB), F32), None, None, (pad, F32), (pad, F32)]
    scratch += [((FLUX, 32, COLS), F32), ((FLUX, ROWS, COLS), F32), (band, F32), (band, ints), (band, F32)]
    scratch += [((VECS * ROWS, VECS * ROWS), F32), ((2, FLUX, 8, 128), F32), ((8, FLUX, ROWS, 128), F32)]
    scratch += [((TILES, FLUX, CAP, 128), F32)] * 2 + [((FLUX * NB, 128), F32)]
    scratch += [((VECS, FLUX, 2, 8, 128), F32)] + [((2, FLUX, 8, 128), F32)] * 2 + [((2, 8, 128), F32)] * 2
    scratch += [((FLUX, 2, 8, 128), F32)]
    scratch += [((1, 128), F32)] * 2 + [((TILES // 2, 1, 128), F32)] + [((1, 128), F32)] * 2
    scratch = [pltpu.VMEM(*v) if v else None for v in scratch]
    scratch[2] = pltpu.SMEM((LEV, LEV), F32)
    scratch[3] = pltpu.SMEM((CAP, TILES), ints)
    x2, basis_v, result = pl.pallas_call(
        kernel,
        out_shape=(
            jax.ShapeDtypeStruct((LEV, ROWS, COLS), F32),
            jax.ShapeDtypeStruct((VECS, LEV, ROWS, COLS), BF16),
            jax.ShapeDtypeStruct((SEG + 8, 128), F32),
        ),
        in_specs=[pl.BlockSpec(memory_space=pltpu.HBM)] * 8,
        out_specs=(vmem,) * 3,
        scratch_shapes=scratch + [dma((9,)), dma(()), dma((GROUPS,)), dma((3, 4)), dma((6,))],
        compiler_params=pltpu.CompilerParams(
            collective_id=0, has_side_effects=True, vmem_limit_bytes=24 << 20
        ),
        name="interval",
    )(
        *(
            pltpu.with_memory_space_constraint(v, pltpu.HBM)
            for v in (
                state,
                basis,
                kappa,
                land_mask,
                jnp.swapaxes(recv_slots, 2, 3),
                jnp.swapaxes(recv_weights, 2, 3),
                vmix,
                jnp.swapaxes(send_rows, 2, 3),
            )
        )
    )
    return pl.pallas_call(
        finish,
        out_shape=(
            jax.ShapeDtypeStruct((1, LEV, ROWS, COLS), F32),
            jax.ShapeDtypeStruct((VECS,), F32),
        ),
        in_specs=[vmem] * 3,
        out_specs=(pl.BlockSpec(memory_space=pl.ANY),) * 2,
        scratch_shapes=[pltpu.VMEM((LEV, ROWS, COLS), F32), pltpu.VMEM((VECS,), F32), dma(()), dma(())],
        compiler_params=pltpu.CompilerParams(vmem_limit_bytes=16 << 20),
        name="finish",
    )(x2, basis_v, result)


def solution(mesh):
    return jax.shard_map(
        body,
        mesh=mesh,
        in_specs=(
            P("comp", None, "tile", None),
            P(None, "comp", None, "tile", None),
            P("comp", "tile", None),
            P("comp", None, None),
            P("tile", None),
            P("comp", "tile", None, None),
            P("comp", "tile", None, None),
            P("comp", "tile", None, None),
        ),
        out_specs=(P("comp", None, "tile", None), P()),
        check_vma=False,
    )
```

```python
import functools

import jax
import jax.numpy as jnp
from jax import lax
from jax.experimental import pallas as pl
from jax.experimental.pallas import tpu as pltpu
from jax.sharding import PartitionSpec as P

FLUX = 4
VECS = 12
LEV = 8
ROWS = 16
COLS = 1024
TILES = 64
CAP = 8
NB = 128
GROUPS = 4
PER = TILES // GROUPS
MESH = pl.DeviceIdType.MESH
F32 = jnp.float32
BF16 = jnp.bfloat16
SEG = 16


def hops(k):
    return sum((0, 1, 2, 1)[(k >> s) & 3] for s in (0, 2, 4))


FAR_FIRST = sorted(range(TILES), key=lambda k: -hops(k))


FAR = [k for k in FAR_FIRST if hops(k) >= 5]
NEAR = [k for k in FAR_FIRST if 0 < hops(k) < 5]


def offset_of(step):
    a, b, c = step & 3, (step >> 2) & 3, step >> 4
    return a, (b - a) & 3, (a + c) & 3


def moved_tile(tile, step):
    dx, dy, dz = offset_of(step)
    return ((tile & 3) + dx & 3) | (((tile >> 2 & 3) + dy & 3) << 2) | (((tile >> 4) + dz & 3) << 4)


def remote(src, dst, send, recv, comp, tile):
    return pltpu.make_async_remote_copy(
        src_ref=src, dst_ref=dst, send_sem=send, recv_sem=recv, device_id=(comp, tile), device_id_type=MESH
    )


def wait_bytes(ref, sem):
    pltpu.make_async_copy(ref, ref, sem).wait()


def sum_over_devices(comp, tile, mine, pair, chip, far, near, sems, meanwhile):
    first = remote(mine, pair, sems.at[0], sems.at[1], 1 - comp, tile)
    first.start()
    for i, k in enumerate(FAR):
        for c in (0, 1):
            remote(mine, far.at[pl.ds(2 * i + comp, 1)], sems.at[2], sems.at[3], c, tile ^ k).start()
    first.wait()
    chip[...] = mine[...] + pair[...]
    own = pl.ds(tile, 1)
    for core in (0, 1):

        @pl.when(comp == core)
        def _():
            for k in NEAR[core::2]:
                for c in (0, 1):
                    remote(chip, near.at[own], sems.at[4], sems.at[5], c, tile ^ k).start()

    near[own] = chip[...]
    meanwhile()
    wait_bytes(far.at[pl.ds(0, 2 * len(FAR))], sems.at[3])
    for i, k in enumerate(FAR):
        near[pl.ds(tile ^ k, 1)] = far[2 * i : 2 * i + 1] + far[2 * i + 1 : 2 * i + 2]
    wait_bytes(near.at[pl.ds(0, len(NEAR))], sems.at[5])
    total = jnp.sum(near[...], axis=0, keepdims=True)
    return total


def wait_sums(far, near, sems):
    wait_bytes(far.at[pl.ds(0, 2 * len(FAR))], sems.at[2])
    wait_bytes(near.at[pl.ds(0, len(NEAR))], sems.at[4])


def stencil(ref, level, kap):
    x = ref[level, 8:24, :]
    lap = (
        ref[level, 7:23, :]
        + ref[level, 9:25, :]
        + pltpu.roll(x, 1, 1)
        + pltpu.roll(x, COLS - 1, 1)
        - 4.0 * x
    )
    return x + kap * lap


def mixed(ref, vmix, level, terms):
    total = vmix[level, 0] * ref[0, 8:24, :]
    for m in range(1, terms):
        total = total + vmix[level, m] * ref[m, 8:24, :]
    return total


def kernel(
    state, basis, kappa, land, slots_hbm, weights_hbm, vmix_hbm, rows_hbm,
    x2, basis_v, result,
    slots, weights, vmix, rows, x0, x1, fh, f, kap, land_v, maskf, gram_v, edge_x,
    surf, bucket, arrived, imp, edge_b, edge_out, edge_in, edge_k, edge_m, near,
    e_mine, e_pair, e_chip, e_far, e_near,
    load, send, recv, halo, esem,
):
    comp = lax.axis_index("comp")
    tile = lax.axis_index("tile")
    total = float(LEV * ROWS * COLS * TILES * 2)
    above = tile - 1 & TILES - 1
    below = tile + 1 & TILES - 1
    every = range(8)

    barrier = pltpu.get_barrier_semaphore()

    def greet(ks):
        for k in ks:
            pl.semaphore_signal(barrier, inc=1, device_id=(1 - comp, tile ^ k), device_id_type=MESH)

    greet(FAR_FIRST[:32])
    surf_loads = [
        pltpu.make_async_copy(
            state.at[0, pl.ds(0, FLUX), :, pl.ds(128 * j, 128)], surf.at[j], load.at[0]
        )
        for j in every
    ]
    rows_load = pltpu.make_async_copy(rows_hbm.at[0, 0], rows, load.at[5])
    x_load = pltpu.make_async_copy(state.at[0], x0.at[:, pl.ds(8, ROWS), :], load.at[1])
    for c in [rows_load, x_load, *surf_loads]:
        c.start()
    greet(FAR_FIRST[32:])
    for t in (above, below):
        pl.semaphore_signal(barrier, inc=1, device_id=(comp, t), device_id_type=MESH)
    kap_load = pltpu.make_async_copy(kappa.at[0], kap, load.at[2])
    kap_load.start()
    land_load = pltpu.make_async_copy(land, land_v, load.at[3])
    land_load.start()
    vmix_load = pltpu.make_async_copy(vmix_hbm.at[0], vmix, load.at[6])
    vmix_load.start()
    table_loads = [
        pltpu.make_async_copy(slots_hbm.at[0, 0], slots, load.at[7]),
        pltpu.make_async_copy(weights_hbm.at[0, 0], weights, load.at[8]),
    ]
    for c in table_loads:
        c.start()
    basis_load = pltpu.make_async_copy(basis.at[:, 0], basis_v, load.at[4])
    basis_load.start()
    rows_load.wait()
    x_load.wait()
    for c in surf_loads:
        c.wait()
    pl.semaphore_wait(barrier, TILES + 2)

    def when_above(f):
        pl.when(tile > 0)(f)

    def when_below(f):
        pl.when(tile < TILES - 1)(f)

    def start_pair(up, down):
        when_above(up.start)
        when_below(down.start)
        return up, down

    def wait_pair(up, down):
        when_below(up.wait_recv)
        when_above(down.wait_recv)
        when_above(up.wait_send)
        when_below(down.wait_send)

    def swap_rows(ref, sems):
        return start_pair(
            remote(ref.at[:, pl.ds(8, 1), :], ref.at[:, pl.ds(24, 1), :], sems.at[0], sems.at[1], comp, above),
            remote(ref.at[:, pl.ds(23, 1), :], ref.at[:, pl.ds(7, 1), :], sems.at[2], sems.at[3], comp, below),
        )

    def clear_ends(ref):
        n = ref.shape[0]

        @pl.when(tile == 0)
        def _():
            ref[:, 7:8, :] = jnp.zeros((n, 1, COLS), F32)

        @pl.when(tile == TILES - 1)
        def _():
            ref[:, 24:25, :] = jnp.zeros((n, 1, COLS), F32)

    swap = swap_rows(x0, halo.at[0])

    flat_surf = surf.reshape(8 * FLUX * ROWS, 128)
    flat_bucket = bucket.reshape(TILES * FLUX * CAP, 128)

    def deliver(step, carry):
        dest = moved_tile(tile, step)
        for j in range(CAP):
            blk = rows[j, dest]
            start = (blk & 7) * (FLUX * ROWS) + (blk >> 3)
            flat_bucket[pl.ds(step * (FLUX * CAP) + j, FLUX, stride=CAP), :] = flat_surf[
                pl.ds(start, FLUX, stride=ROWS), :
            ]
        remote(bucket.at[step], arrived.at[step], send, recv.at[step >> 4], 1 - comp, dest).start()
        return carry

    lax.fori_loop(0, TILES // 2, deliver, 0)

    vmix_load.wait()
    kap_load.wait()
    land_load.wait()
    maskf[...] = jnp.where(comp == 0, land_v[...].astype(F32), jnp.ones((ROWS, COLS), F32))
    wait_pair(*swap)
    clear_ends(x0)
    for l in range(LEV):
        x1[l, 8:24, :] = maskf[...] * (stencil(x0, l, kap[...]) + mixed(x0, vmix, l, LEV))
    deep = x1.at[pl.ds(FLUX, LEV - FLUX)]
    for row in (7, 24):
        x1[0:FLUX, row : row + 1, :] = jnp.zeros((FLUX, 1, COLS), F32)
        fh[:, row : row + 1, :] = jnp.zeros((FLUX, 1, COLS), F32)
    swap = swap_rows(deep, halo.at[1])
    lax.fori_loop(TILES // 2, TILES, deliver, 0)

    for j in every:
        cut = slice(j * 128, (j + 1) * 128)
        for end, row in ((0, 0), (1, 15)):
            m = maskf[row : row + 1, cut]
            edge_m[end, j : j + 1] = m
            edge_k[end, j : j + 1] = m * kap[row : row + 1, cut]
            for l in range(FLUX):
                edge_x[end, l, j : j + 1] = x1[l, 8 + row : 9 + row, cut]
    for l in range(FLUX):
        x2[l] = maskf[...] * (stencil(x1, l, kap[...]) + mixed(x1, vmix, l, LEV))

    for c in table_loads:
        c.wait()
    slot = slots[...]
    src = slot >> 3
    a = (tile & 3) - (src & 3) & 3
    b = (tile >> 2 & 3) - (src >> 2 & 3) + a & 3
    c = (tile >> 4) - (src >> 4) - a & 3
    place = (a | b << 2 | c << 4) * CAP + (slot & 7)
    table = jnp.concatenate([place.astype(F32), weights[...], jnp.zeros((NB - 8, NB), F32)], axis=0).T
    at_lane = lax.broadcasted_iota(jnp.int32, (NB, TILES * CAP), 1).astype(F32)
    matrix = jnp.zeros((NB, TILES * CAP), F32)
    for k in range(4):
        matrix = matrix + jnp.where(at_lane == table[:, k : k + 1], table[:, 4 + k : 5 + k], 0.0)
    ends = jnp.concatenate([matrix[:8], matrix[-8:]], axis=0)

    def halves(v):
        high = v.astype(BF16)
        return high, (v - high.astype(F32)).astype(BF16)

    high, low = halves(matrix)
    ends_high, ends_low = halves(ends)

    basis_load.wait()
    lane = lax.broadcasted_iota(jnp.int32, (SEG, 128), 1)
    sub = lax.broadcasted_iota(jnp.int32, (SEG, 128), 0)

    def gram_step(n, acc):
        level = n >> 2
        at = pl.multiple_of((n & 3) * 256, 256)
        x = jnp.concatenate([basis_v[i, level, :, pl.ds(at, 256)] for i in range(VECS)], axis=0)
        gram_v[...] += lax.dot_general(x, x, (((1,), (1,)), ((), ())), preferred_element_type=F32)
        return acc

    span = VECS * ROWS
    gram_v[...] = jnp.zeros((span, span), F32)
    lax.fori_loop(0, 32, gram_step, 0)
    row_of = lax.broadcasted_iota(jnp.int32, (ROWS, span), 0)
    col_of = lax.broadcasted_iota(jnp.int32, (ROWS, span), 1)
    diagonal = row_of == (col_of & ROWS - 1)
    picked = [
        jnp.sum(jnp.where(diagonal, gram_v[i * ROWS : (i + 1) * ROWS, :], 0.0), axis=0, keepdims=True)
        for i in range(VECS)
    ]
    picked = jnp.concatenate(picked + [jnp.zeros((SEG - VECS, span), F32)], axis=0)
    gather = lax.broadcasted_iota(jnp.int32, (span, 128), 0) >> 4 == lax.broadcasted_iota(jnp.int32, (span, 128), 1)
    square = jnp.dot(picked, gather.astype(F32), precision=lax.Precision.HIGHEST, preferred_element_type=F32)
    empty = jnp.zeros((1, 128), F32)

    def to_lanes(rows_, k):
        stack = jnp.concatenate(rows_ + [empty] * (SEG - len(rows_)), axis=0)
        return jnp.where(lane == sub + SEG * k, jnp.sum(stack, axis=1, keepdims=True), 0.0)

    gram = jnp.zeros((SEG, 128), F32)
    for k in range(VECS // 2 + 1):
        other = jnp.where(sub + k >= VECS, sub + k - VECS, sub + k)
        own = sub < (VECS if k < VECS // 2 else VECS // 2)
        col = jnp.sum(jnp.where((lane == other) & own, square, 0.0), axis=1, keepdims=True)
        gram = gram + jnp.where(lane == sub + SEG * k, col, 0.0)

    wait_pair(*swap)
    clear_ends(deep)
    for l in range(FLUX, LEV):
        x2[l] = maskf[...] * (stencil(x1, l, kap[...]) + mixed(x1, vmix, l, LEV))

    def edge_step(i, carry):
        for l in range(FLUX):
            for j in every:
                v = basis_v[i, l, :, j * 128 : (j + 1) * 128].astype(F32)
                edge_b[i, l, 0, j : j + 1] = v[:1]
                edge_b[i, l, 1, j : j + 1] = v[15:]
        return carry

    lax.fori_loop(0, VECS, edge_step, 0)

    dot = functools.partial(jnp.dot, preferred_element_type=F32)

    def group(g):
        wait_bytes(arrived.at[pl.ds(g * PER, PER)], recv.at[g])
        got = jnp.concatenate(
            [arrived[g * PER : (g + 1) * PER, i].reshape(PER * CAP, 128) for i in range(FLUX)], axis=1
        )
        return slice(g * PER * CAP, (g + 1) * PER * CAP), *halves(got)

    def times(high, low, cut, got_high, got_low):
        return dot(high[:, cut], got_high) + dot(low[:, cut], got_high) + dot(high[:, cut], got_low)

    sums = jnp.zeros((NB, FLUX * 128), F32)
    for g in range(GROUPS - 1):
        sums = sums + times(high, low, *group(g))
    tail = group(GROUPS - 1)
    border = jnp.concatenate([sums[:8], sums[-8:]], axis=0) + times(ends_high, ends_low, *tail)
    for end in (0, 1):
        for i in range(FLUX):
            edge_out[end, i] = edge_x[end, i] + edge_m[end] * border[end * 8 : end * 8 + 8, i * 128 : (i + 1) * 128]
    edges = start_pair(
        remote(edge_out.at[0], edge_in.at[1], halo.at[2, 0], halo.at[2, 1], comp, above),
        remote(edge_out.at[1], edge_in.at[0], halo.at[2, 2], halo.at[2, 3], comp, below),
    )
    sums = sums + times(high, low, *tail)
    for i in range(FLUX):
        imp[i * NB : (i + 1) * NB, :] = sums[:, i * 128 : (i + 1) * 128]
    for i in range(FLUX):
        for j in every:
            cut = slice(j * 128, (j + 1) * 128)
            piece = imp[pl.ds(i * NB + j, ROWS, stride=8), :]
            f[i, :, cut] = piece
            fh[i, 8:24, cut] = maskf[:, cut] * piece
    for l in range(LEV):
        z = mixed(fh, vmix, l, FLUX)
        if l < FLUX:
            z = z + stencil(fh, l, kap[...]) + f[l]
        x2[l] = x2[l] + maskf[...] * z

    def dot_step(n, acc):
        level = n >> 2
        for half in (0, 1):
            at = pl.multiple_of((n & 3) * 256 + half * 128, 128)
            x = x2[level, :, pl.ds(at, 128)]
            out = [a + basis_v[i, level, :, pl.ds(at, 128)].astype(F32) * x for i, a in enumerate(acc[:VECS])]
            acc = tuple(out) + (acc[VECS] + x * x,)
        return acc

    acc = lax.fori_loop(0, 32, dot_step, tuple(jnp.zeros((16, 128), F32) for _ in range(VECS + 1)))
    acc = [a[:8] + a[8:] for a in acc]
    for l in range(FLUX):
        for end, row in ((0, 0), (1, 15)):
            for j in every:
                near[l, end, j : j + 1] = x2[l, row : row + 1, j * 128 : (j + 1) * 128]
    wait_pair(*edges)
    extra = {}
    for end, last in ((0, 0), (1, TILES - 1)):
        for l in range(FLUX):
            add = jnp.where(tile == last, jnp.zeros((8, 128), F32), edge_k[end] * edge_in[end, l])
            extra[l, end] = add
            for i in range(VECS):
                acc[i] = acc[i] + edge_b[i, l, end] * add
            acc[VECS] = acc[VECS] + add * (2.0 * near[l, end] + add)
    sums_of = [jnp.sum(a, axis=0, keepdims=True) for a in acc]
    e_mine[...] = jnp.sum(gram + to_lanes(sums_of, 7), axis=0, keepdims=True)

    def add_edges():
        for (l, end), add in extra.items():
            row = 15 * end
            full = near[l, end] + add
            for j in every:
                x2[l, row : row + 1, j * 128 : (j + 1) * 128] = full[j : j + 1]

    dots = sum_over_devices(comp, tile, e_mine, e_pair, e_chip, e_far, e_near, esem, add_edges)

    one = lax.broadcasted_iota(jnp.int32, (1, 128), 1)
    seg, pos = one >> 4, one & 15
    vals = jnp.where((seg == 7) & (pos < VECS), dots * (1.0 / total), 0.0)
    coef = pltpu.roll(vals, SEG, 1)
    twice = coef + pltpu.roll(coef, VECS, 1)
    left = jnp.zeros((1, 128), F32)
    right = jnp.zeros((1, 128), F32)
    for k in range(VECS // 2 + 1):
        left = jnp.where(seg == k, pltpu.roll(coef, SEG * k, 1) if k else coef, left)
        right = jnp.where(seg == k, pltpu.roll(twice, (SEG - 1) * k, 1) if k else twice, right)
    factor = jnp.where(seg == 0, 1.0, 2.0)
    products = jnp.where((seg < 7) & (pos < VECS), factor * dots * left * right, 0.0)
    square = jnp.where((seg == 7) & (pos == VECS), dots, 0.0) - 2.0 * dots * vals + products
    square = jnp.sum(square, axis=1, keepdims=True)
    scale = 1.0 / jnp.sqrt(jnp.maximum(square, 0.0) * (1.0 / total) + 1e-06)
    line = jnp.where(one == VECS, 1.0, coef)
    column = jnp.sum(jnp.where(lane == sub, jnp.broadcast_to(line, (SEG, 128)), 0.0), axis=1, keepdims=True)
    result[0:SEG] = jnp.broadcast_to(column * scale, (SEG, 128))
    result[SEG : SEG + 1] = coef
    wait_sums(e_far, e_near, esem)
    wait_bytes(bucket, send)


def finish(x2, basis_v, result, direction, coefs, out, line, store, small):
    line[...] = result[SEG, :VECS]
    first = pltpu.make_async_copy(line, coefs, small)
    first.start()
    weigh = [jnp.broadcast_to(result[i : i + 1], (ROWS, 128)) for i in range(VECS + 1)]
    for l in range(LEV):

        def part(n, carry):
            for half in (0, 1):
                at = pl.multiple_of(n * 256 + half * 128, 128)
                w = weigh[VECS] * x2[l, :, pl.ds(at, 128)]
                for i in range(VECS):
                    w = w - weigh[i] * basis_v[i, l, :, pl.ds(at, 128)].astype(F32)
                out[l, :, pl.ds(at, 128)] = w
            return carry

        lax.fori_loop(0, 4, part, 0)
        pltpu.make_async_copy(out.at[l], direction.at[0, l], store).start()
    first.wait()
    wait_bytes(out, store)


def body(state, basis, kappa, vmix, land_mask, send_rows, recv_slots, recv_weights):
    vmem = pl.BlockSpec(memory_space=pltpu.VMEM)
    dma = pltpu.SemaphoreType.DMA
    pad = (LEV, 32, COLS)
    band = (ROWS, COLS)
    ints = jnp.int32
    scratch = [((4, NB), ints), ((4, NB), F32), None, None, (pad, F32), (pad, F32)]
    scratch += [((FLUX, 32, COLS), F32), ((FLUX, ROWS, COLS), F32), (band, F32), (band, ints), (band, F32)]
    scratch += [((VECS * ROWS, VECS * ROWS), F32), ((2, FLUX, 8, 128), F32), ((8, FLUX, ROWS, 128), F32)]
    scratch += [((TILES, FLUX, CAP, 128), F32)] * 2 + [((FLUX * NB, 128), F32)]
    scratch += [((VECS, FLUX, 2, 8, 128), F32)] + [((2, FLUX, 8, 128), F32)] * 2 + [((2, 8, 128), F32)] * 2
    scratch += [((FLUX, 2, 8, 128), F32)]
    scratch += [((1, 128), F32)] * 3 + [((16, 128), F32), ((TILES, 128), F32)]
    scratch = [pltpu.VMEM(*v) if v else None for v in scratch]
    scratch[2] = pltpu.SMEM((LEV, LEV), F32)
    scratch[3] = pltpu.SMEM((CAP, TILES), ints)
    x2, basis_v, result = pl.pallas_call(
        kernel,
        out_shape=(
            jax.ShapeDtypeStruct((LEV, ROWS, COLS), F32),
            jax.ShapeDtypeStruct((VECS, LEV, ROWS, COLS), BF16),
            jax.ShapeDtypeStruct((SEG + 8, 128), F32),
        ),
        in_specs=[pl.BlockSpec(memory_space=pltpu.HBM)] * 8,
        out_specs=(vmem,) * 3,
        scratch_shapes=scratch + [dma((9,)), dma(()), dma((GROUPS,)), dma((3, 4)), dma((6,))],
        compiler_params=pltpu.CompilerParams(
            collective_id=0, has_side_effects=True, vmem_limit_bytes=24 << 20
        ),
        name="interval",
    )(
        *(
            pltpu.with_memory_space_constraint(v, pltpu.HBM)
            for v in (
                state,
                basis,
                kappa,
                land_mask,
                jnp.swapaxes(recv_slots, 2, 3),
                jnp.swapaxes(recv_weights, 2, 3),
                vmix,
                jnp.swapaxes(send_rows, 2, 3),
            )
        )
    )
    return pl.pallas_call(
        finish,
        out_shape=(
            jax.ShapeDtypeStruct((1, LEV, ROWS, COLS), F32),
            jax.ShapeDtypeStruct((VECS,), F32),
        ),
        in_specs=[vmem] * 3,
        out_specs=(pl.BlockSpec(memory_space=pl.ANY),) * 2,
        scratch_shapes=[pltpu.VMEM((LEV, ROWS, COLS), F32), pltpu.VMEM((VECS,), F32), dma(()), dma(())],
        compiler_params=pltpu.CompilerParams(vmem_limit_bytes=16 << 20),
        name="finish",
    )(x2, basis_v, result)


def solution(mesh):
    return jax.shard_map(
        body,
        mesh=mesh,
        in_specs=(
            P("comp", None, "tile", None),
            P(None, "comp", None, "tile", None),
            P("comp", "tile", None),
            P("comp", None, None),
            P("tile", None),
            P("comp", "tile", None, None),
            P("comp", "tile", None, None),
            P("comp", "tile", None, None),
        ),
        out_specs=(P("comp", None, "tile", None), P()),
        check_vma=False,
    )
```

```python
import functools

import jax
import jax.numpy as jnp
from jax import lax
from jax.experimental import pallas as pl
from jax.experimental.pallas import tpu as pltpu
from jax.sharding import PartitionSpec as P

FLUX = 4
VECS = 12
LEV = 8
ROWS = 16
COLS = 1024
TILES = 64
CAP = 8
NB = 128
GROUPS = 4
PER = TILES // GROUPS
EARLY = 48
MESH = pl.DeviceIdType.MESH
F32 = jnp.float32
BF16 = jnp.bfloat16
SEG = 16


def hops(k):
    return sum((0, 1, 2, 1)[(k >> s) & 3] for s in (0, 2, 4))


FAR_FIRST = sorted(range(TILES), key=lambda k: -hops(k))


FAR = [k for k in FAR_FIRST if hops(k) >= 5]
NEAR = [k for k in FAR_FIRST if 0 < hops(k) < 5]


def offset_of(step):
    a, b, c = step & 3, (step >> 2) & 3, step >> 4
    return a, (b - a) & 3, (a + c) & 3


def moved_tile(tile, step):
    dx, dy, dz = offset_of(step)
    return ((tile & 3) + dx & 3) | (((tile >> 2 & 3) + dy & 3) << 2) | (((tile >> 4) + dz & 3) << 4)


def remote(src, dst, send, recv, comp, tile):
    return pltpu.make_async_remote_copy(
        src_ref=src, dst_ref=dst, send_sem=send, recv_sem=recv, device_id=(comp, tile), device_id_type=MESH
    )


def wait_bytes(ref, sem):
    pltpu.make_async_copy(ref, ref, sem).wait()


def sum_over_devices(comp, tile, mine, pair, chip, far, near, sems, meanwhile):
    first = remote(mine, pair, sems.at[0], sems.at[1], 1 - comp, tile)
    first.start()
    for i, k in enumerate(FAR):
        for c in (0, 1):
            remote(mine, far.at[pl.ds(2 * i + comp, 1)], sems.at[2], sems.at[3], c, tile ^ k).start()
    first.wait()
    chip[...] = mine[...] + pair[...]
    own = pl.ds(tile, 1)
    for core in (0, 1):

        @pl.when(comp == core)
        def _():
            for k in NEAR[core::2]:
                for c in (0, 1):
                    remote(chip, near.at[own], sems.at[4], sems.at[5], c, tile ^ k).start()

    near[own] = chip[...]
    meanwhile()
    wait_bytes(far.at[pl.ds(0, 2 * len(FAR))], sems.at[3])
    for i, k in enumerate(FAR):
        near[pl.ds(tile ^ k, 1)] = far[2 * i : 2 * i + 1] + far[2 * i + 1 : 2 * i + 2]
    wait_bytes(near.at[pl.ds(0, len(NEAR))], sems.at[5])
    total = jnp.sum(near[...], axis=0, keepdims=True)
    return total


def wait_sums(far, near, sems):
    wait_bytes(far.at[pl.ds(0, 2 * len(FAR))], sems.at[2])
    wait_bytes(near.at[pl.ds(0, len(NEAR))], sems.at[4])


def stencil(ref, level, kap):
    x = ref[level, 8:24, :]
    lap = (
        ref[level, 7:23, :]
        + ref[level, 9:25, :]
        + pltpu.roll(x, 1, 1)
        + pltpu.roll(x, COLS - 1, 1)
        - 4.0 * x
    )
    return x + kap * lap


def mixed(ref, vmix, level, terms):
    total = vmix[level, 0] * ref[0, 8:24, :]
    for m in range(1, terms):
        total = total + vmix[level, m] * ref[m, 8:24, :]
    return total


def kernel(
    state, basis, kappa, land, slots_hbm, weights_hbm, vmix_hbm, rows_hbm,
    x2, wide, result,
    slots, weights, vmix, rows, x0, x1, fh, f, kap, land_v, maskf, gram_v, edge_x,
    basis_v, surf, bucket, arrived, imp, edge_b, edge_out, edge_in, edge_k, edge_m, near,
    e_mine, e_pair, e_chip, e_far, e_near,
    load, send, recv, halo, esem,
):
    comp = lax.axis_index("comp")
    tile = lax.axis_index("tile")
    total = float(LEV * ROWS * COLS * TILES * 2)
    above = tile - 1 & TILES - 1
    below = tile + 1 & TILES - 1
    every = range(8)

    barrier = pltpu.get_barrier_semaphore()

    def greet(ks):
        for k in ks:
            pl.semaphore_signal(barrier, inc=1, device_id=(1 - comp, tile ^ k), device_id_type=MESH)

    surf_loads = [
        pltpu.make_async_copy(
            state.at[0, pl.ds(0, FLUX), :, pl.ds(128 * j, 128)], surf.at[j], load.at[0]
        )
        for j in every
    ]
    rows_load = pltpu.make_async_copy(rows_hbm.at[0, 0], rows, load.at[5])
    x_load = pltpu.make_async_copy(state.at[0], x0.at[:, pl.ds(8, ROWS), :], load.at[1])
    greet(FAR_FIRST)
    for c in [rows_load, *surf_loads]:
        c.start()
    for t in (above, below):
        pl.semaphore_signal(barrier, inc=1, device_id=(comp, t), device_id_type=MESH)
    x_load.start()
    kap_load = pltpu.make_async_copy(kappa.at[0], kap, load.at[2])
    kap_load.start()
    land_load = pltpu.make_async_copy(land, land_v, load.at[3])
    land_load.start()
    vmix_load = pltpu.make_async_copy(vmix_hbm.at[0], vmix, load.at[6])
    vmix_load.start()
    table_loads = [
        pltpu.make_async_copy(slots_hbm.at[0, 0], slots, load.at[7]),
        pltpu.make_async_copy(weights_hbm.at[0, 0], weights, load.at[8]),
    ]
    for c in table_loads:
        c.start()
    basis_load = pltpu.make_async_copy(basis.at[:, 0], basis_v, load.at[4])
    rows_load.wait()
    x_load.wait()
    for c in surf_loads:
        c.wait()
    pl.semaphore_wait(barrier, TILES + 2)

    def when_above(f):
        pl.when(tile > 0)(f)

    def when_below(f):
        pl.when(tile < TILES - 1)(f)

    def start_pair(up, down):
        when_above(up.start)
        when_below(down.start)
        return up, down

    def wait_pair(up, down):
        when_below(up.wait_recv)
        when_above(down.wait_recv)
        when_above(up.wait_send)
        when_below(down.wait_send)

    def swap_rows(ref, sems):
        return start_pair(
            remote(ref.at[:, pl.ds(8, 1), :], ref.at[:, pl.ds(24, 1), :], sems.at[0], sems.at[1], comp, above),
            remote(ref.at[:, pl.ds(23, 1), :], ref.at[:, pl.ds(7, 1), :], sems.at[2], sems.at[3], comp, below),
        )

    def clear_ends(ref):
        n = ref.shape[0]

        @pl.when(tile == 0)
        def _():
            ref[:, 7:8, :] = jnp.zeros((n, 1, COLS), F32)

        @pl.when(tile == TILES - 1)
        def _():
            ref[:, 24:25, :] = jnp.zeros((n, 1, COLS), F32)

    swap = swap_rows(x0, halo.at[0])

    flat_surf = surf.reshape(8 * FLUX * ROWS, 128)
    flat_bucket = bucket.reshape(TILES * FLUX * CAP, 128)

    def deliver(step, carry):
        dest = moved_tile(tile, step)
        for j in range(CAP):
            blk = rows[j, dest]
            start = (blk & 7) * (FLUX * ROWS) + (blk >> 3)
            flat_bucket[pl.ds(step * (FLUX * CAP) + j, FLUX, stride=CAP), :] = flat_surf[
                pl.ds(start, FLUX, stride=ROWS), :
            ]
        remote(bucket.at[step], arrived.at[step], send, recv.at[step >> 4], 1 - comp, dest).start()
        return carry

    basis_load.start()
    lax.fori_loop(0, EARLY, deliver, 0)

    vmix_load.wait()
    kap_load.wait()
    land_load.wait()
    maskf[...] = jnp.where(comp == 0, land_v[...].astype(F32), jnp.ones((ROWS, COLS), F32))
    wait_pair(*swap)
    clear_ends(x0)
    for l in range(LEV):
        x1[l, 8:24, :] = maskf[...] * (stencil(x0, l, kap[...]) + mixed(x0, vmix, l, LEV))
    deep = x1.at[pl.ds(FLUX, LEV - FLUX)]
    for row in (7, 24):
        x1[0:FLUX, row : row + 1, :] = jnp.zeros((FLUX, 1, COLS), F32)
        fh[:, row : row + 1, :] = jnp.zeros((FLUX, 1, COLS), F32)
    swap = swap_rows(deep, halo.at[1])
    lax.fori_loop(EARLY, TILES, deliver, 0)

    for j in every:
        cut = slice(j * 128, (j + 1) * 128)
        for end, row in ((0, 0), (1, 15)):
            m = maskf[row : row + 1, cut]
            edge_m[end, j : j + 1] = m
            edge_k[end, j : j + 1] = m * kap[row : row + 1, cut]
            for l in range(FLUX):
                edge_x[end, l, j : j + 1] = x1[l, 8 + row : 9 + row, cut]
    for l in range(FLUX):
        x2[l] = maskf[...] * (stencil(x1, l, kap[...]) + mixed(x1, vmix, l, LEV))

    for c in table_loads:
        c.wait()
    slot = slots[...]
    src = slot >> 3
    a = (tile & 3) - (src & 3) & 3
    b = (tile >> 2 & 3) - (src >> 2 & 3) + a & 3
    c = (tile >> 4) - (src >> 4) - a & 3
    place = (a | b << 2 | c << 4) * CAP + (slot & 7)
    table = jnp.concatenate([place.astype(F32), weights[...], jnp.zeros((NB - 8, NB), F32)], axis=0).T
    at_lane = lax.broadcasted_iota(jnp.int32, (NB, TILES * CAP), 1).astype(F32)
    matrix = jnp.zeros((NB, TILES * CAP), F32)
    for k in range(4):
        matrix = matrix + jnp.where(at_lane == table[:, k : k + 1], table[:, 4 + k : 5 + k], 0.0)
    ends = jnp.concatenate([matrix[:8], matrix[-8:]], axis=0)

    def halves(v):
        high = v.astype(BF16)
        return high, (v - high.astype(F32)).astype(BF16)

    high, low = halves(matrix)
    ends_high, ends_low = halves(ends)

    basis_load.wait()
    lane = lax.broadcasted_iota(jnp.int32, (SEG, 128), 1)
    sub = lax.broadcasted_iota(jnp.int32, (SEG, 128), 0)

    def gram_step(n, acc):
        level = n >> 2
        at = pl.multiple_of((n & 3) * 256, 256)
        x = jnp.concatenate([basis_v[i, level, :, pl.ds(at, 256)] for i in range(VECS)], axis=0)
        gram_v[...] += lax.dot_general(x, x, (((1,), (1,)), ((), ())), preferred_element_type=F32)
        return acc

    span = VECS * ROWS
    gram_v[...] = jnp.zeros((span, span), F32)
    lax.fori_loop(0, 32, gram_step, 0)
    row_of = lax.broadcasted_iota(jnp.int32, (ROWS, span), 0)
    col_of = lax.broadcasted_iota(jnp.int32, (ROWS, span), 1)
    diagonal = row_of == (col_of & ROWS - 1)
    picked = [
        jnp.sum(jnp.where(diagonal, gram_v[i * ROWS : (i + 1) * ROWS, :], 0.0), axis=0, keepdims=True)
        for i in range(VECS)
    ]
    picked = jnp.concatenate(picked + [jnp.zeros((SEG - VECS, span), F32)], axis=0)
    gather = lax.broadcasted_iota(jnp.int32, (span, 128), 0) >> 4 == lax.broadcasted_iota(jnp.int32, (span, 128), 1)
    square = jnp.dot(picked, gather.astype(F32), precision=lax.Precision.HIGHEST, preferred_element_type=F32)
    empty = jnp.zeros((1, 128), F32)

    def to_lanes(rows_, k):
        stack = jnp.concatenate(rows_ + [empty] * (SEG - len(rows_)), axis=0)
        return jnp.where(lane == sub + SEG * k, jnp.sum(stack, axis=1, keepdims=True), 0.0)

    gram = jnp.zeros((SEG, 128), F32)
    for k in range(VECS // 2 + 1):
        other = jnp.where(sub + k >= VECS, sub + k - VECS, sub + k)
        own = sub < (VECS if k < VECS // 2 else VECS // 2)
        col = jnp.sum(jnp.where((lane == other) & own, square, 0.0), axis=1, keepdims=True)
        gram = gram + jnp.where(lane == sub + SEG * k, col, 0.0)

    wait_pair(*swap)
    clear_ends(deep)
    for l in range(FLUX, LEV):
        x2[l] = maskf[...] * (stencil(x1, l, kap[...]) + mixed(x1, vmix, l, LEV))

    def edge_step(i, carry):
        for l in range(FLUX):
            for j in every:
                v = basis_v[i, l, :, j * 128 : (j + 1) * 128].astype(F32)
                edge_b[i, l, 0, j : j + 1] = v[:1]
                edge_b[i, l, 1, j : j + 1] = v[15:]
        return carry

    lax.fori_loop(0, VECS, edge_step, 0)

    dot = functools.partial(jnp.dot, preferred_element_type=F32)

    def group(g):
        wait_bytes(arrived.at[pl.ds(g * PER, PER)], recv.at[g])
        got = jnp.concatenate(
            [arrived[g * PER : (g + 1) * PER, i].reshape(PER * CAP, 128) for i in range(FLUX)], axis=1
        )
        return slice(g * PER * CAP, (g + 1) * PER * CAP), *halves(got)

    def times(high, low, cut, got_high, got_low):
        return dot(high[:, cut], got_high) + dot(low[:, cut], got_high) + dot(high[:, cut], got_low)

    sums = jnp.zeros((NB, FLUX * 128), F32)
    for g in range(GROUPS - 1):
        sums = sums + times(high, low, *group(g))
    tail = group(GROUPS - 1)
    border = jnp.concatenate([sums[:8], sums[-8:]], axis=0) + times(ends_high, ends_low, *tail)
    for end in (0, 1):
        for i in range(FLUX):
            edge_out[end, i] = edge_x[end, i] + edge_m[end] * border[end * 8 : end * 8 + 8, i * 128 : (i + 1) * 128]
    edges = start_pair(
        remote(edge_out.at[0], edge_in.at[1], halo.at[2, 0], halo.at[2, 1], comp, above),
        remote(edge_out.at[1], edge_in.at[0], halo.at[2, 2], halo.at[2, 3], comp, below),
    )
    sums = sums + times(high, low, *tail)
    for i in range(FLUX):
        imp[i * NB : (i + 1) * NB, :] = sums[:, i * 128 : (i + 1) * 128]
    for i in range(FLUX):
        for j in every:
            cut = slice(j * 128, (j + 1) * 128)
            piece = imp[pl.ds(i * NB + j, ROWS, stride=8), :]
            f[i, :, cut] = piece
            fh[i, 8:24, cut] = maskf[:, cut] * piece
    for l in range(LEV):
        z = mixed(fh, vmix, l, FLUX)
        if l < FLUX:
            z = z + stencil(fh, l, kap[...]) + f[l]
        x2[l] = x2[l] + maskf[...] * z

    def dot_step(n, acc):
        level = n >> 2
        for half in (0, 1):
            at = pl.multiple_of((n & 3) * 256 + half * 128, 128)
            x = x2[level, :, pl.ds(at, 128)]
            out = [a + basis_v[i, level, :, pl.ds(at, 128)].astype(F32) * x for i, a in enumerate(acc[:VECS])]
            acc = tuple(out) + (acc[VECS] + x * x,)
        return acc

    acc = lax.fori_loop(0, 32, dot_step, tuple(jnp.zeros((16, 128), F32) for _ in range(VECS + 1)))
    acc = [a[:8] + a[8:] for a in acc]
    for l in range(FLUX):
        for end, row in ((0, 0), (1, 15)):
            for j in every:
                near[l, end, j : j + 1] = x2[l, row : row + 1, j * 128 : (j + 1) * 128]
    wait_pair(*edges)
    extra = {}
    for end, last in ((0, 0), (1, TILES - 1)):
        for l in range(FLUX):
            add = jnp.where(tile == last, jnp.zeros((8, 128), F32), edge_k[end] * edge_in[end, l])
            extra[l, end] = add
            for i in range(VECS):
                acc[i] = acc[i] + edge_b[i, l, end] * add
            acc[VECS] = acc[VECS] + add * (2.0 * near[l, end] + add)
    sums_of = [jnp.sum(a, axis=0, keepdims=True) for a in acc]
    e_mine[...] = jnp.sum(gram + to_lanes(sums_of, 7), axis=0, keepdims=True)

    def widen(i, carry):
        for l in range(LEV):
            wide[i, l] = basis_v[i, l].astype(F32)
        return carry

    def add_edges():
        lax.fori_loop(0, VECS, widen, 0)
        for (l, end), add in extra.items():
            row = 15 * end
            full = near[l, end] + add
            for j in every:
                x2[l, row : row + 1, j * 128 : (j + 1) * 128] = full[j : j + 1]

    dots = sum_over_devices(comp, tile, e_mine, e_pair, e_chip, e_far, e_near, esem, add_edges)

    one = lax.broadcasted_iota(jnp.int32, (1, 128), 1)
    seg, pos = one >> 4, one & 15
    vals = jnp.where((seg == 7) & (pos < VECS), dots * (1.0 / total), 0.0)
    coef = pltpu.roll(vals, SEG, 1)
    twice = coef + pltpu.roll(coef, VECS, 1)
    left = jnp.zeros((1, 128), F32)
    right = jnp.zeros((1, 128), F32)
    for k in range(VECS // 2 + 1):
        left = jnp.where(seg == k, pltpu.roll(coef, SEG * k, 1) if k else coef, left)
        right = jnp.where(seg == k, pltpu.roll(twice, (SEG - 1) * k, 1) if k else twice, right)
    factor = jnp.where(seg == 0, 1.0, 2.0)
    products = jnp.where((seg < 7) & (pos < VECS), factor * dots * left * right, 0.0)
    square = jnp.where((seg == 7) & (pos == VECS), dots, 0.0) - 2.0 * dots * vals + products
    square = jnp.sum(square, axis=1, keepdims=True)
    scale = 1.0 / jnp.sqrt(jnp.maximum(square, 0.0) * (1.0 / total) + 1e-06)
    line = jnp.where(one == VECS, 1.0, coef)
    column = jnp.sum(jnp.where(lane == sub, jnp.broadcast_to(line, (SEG, 128)), 0.0), axis=1, keepdims=True)
    result[0:SEG] = jnp.broadcast_to(column * scale, (SEG, 128))
    result[SEG : SEG + 1] = coef
    wait_sums(e_far, e_near, esem)
    wait_bytes(bucket, send)


def finish(x2, wide, result, direction, coefs, out, line, store, small):
    line[...] = result[SEG, :VECS]
    first = pltpu.make_async_copy(line, coefs, small)
    first.start()
    weigh = [jnp.broadcast_to(result[i : i + 1], (ROWS, 128)) for i in range(VECS + 1)]
    for l in range(LEV):

        def part(n, carry):
            for half in (0, 1):
                at = pl.multiple_of(n * 256 + half * 128, 128)
                w = weigh[VECS] * x2[l, :, pl.ds(at, 128)]
                for i in range(VECS):
                    w = w - weigh[i] * wide[i, l, :, pl.ds(at, 128)]
                out[l, :, pl.ds(at, 128)] = w
            return carry

        lax.fori_loop(0, 4, part, 0)
        pltpu.make_async_copy(out.at[l], direction.at[0, l], store).start()
    first.wait()
    wait_bytes(out, store)


def body(state, basis, kappa, vmix, land_mask, send_rows, recv_slots, recv_weights):
    vmem = pl.BlockSpec(memory_space=pltpu.VMEM)
    dma = pltpu.SemaphoreType.DMA
    pad = (LEV, 32, COLS)
    band = (ROWS, COLS)
    ints = jnp.int32
    scratch = [((4, NB), ints), ((4, NB), F32), None, None, (pad, F32), (pad, F32)]
    scratch += [((FLUX, 32, COLS), F32), ((FLUX, ROWS, COLS), F32), (band, F32), (band, ints), (band, F32)]
    scratch += [((VECS * ROWS, VECS * ROWS), F32), ((2, FLUX, 8, 128), F32)]
    scratch += [((VECS, LEV, ROWS, COLS), BF16), ((8, FLUX, ROWS, 128), F32)]
    scratch += [((TILES, FLUX, CAP, 128), F32)] * 2 + [((FLUX * NB, 128), F32)]
    scratch += [((VECS, FLUX, 2, 8, 128), F32)] + [((2, FLUX, 8, 128), F32)] * 2 + [((2, 8, 128), F32)] * 2
    scratch += [((FLUX, 2, 8, 128), F32)]
    scratch += [((1, 128), F32)] * 3 + [((16, 128), F32), ((TILES, 128), F32)]
    scratch = [pltpu.VMEM(*v) if v else None for v in scratch]
    scratch[2] = pltpu.SMEM((LEV, LEV), F32)
    scratch[3] = pltpu.SMEM((CAP, TILES), ints)
    x2, wide, result = pl.pallas_call(
        kernel,
        out_shape=(
            jax.ShapeDtypeStruct((LEV, ROWS, COLS), F32),
            jax.ShapeDtypeStruct((VECS, LEV, ROWS, COLS), F32),
            jax.ShapeDtypeStruct((SEG + 8, 128), F32),
        ),
        in_specs=[pl.BlockSpec(memory_space=pltpu.HBM)] * 8,
        out_specs=(vmem,) * 3,
        scratch_shapes=scratch + [dma((9,)), dma(()), dma((GROUPS,)), dma((3, 4)), dma((6,))],
        compiler_params=pltpu.CompilerParams(
            collective_id=0, has_side_effects=True, vmem_limit_bytes=24 << 20
        ),
        name="interval",
    )(
        *(
            pltpu.with_memory_space_constraint(v, pltpu.HBM)
            for v in (
                state,
                basis,
                kappa,
                land_mask,
                jnp.swapaxes(recv_slots, 2, 3),
                jnp.swapaxes(recv_weights, 2, 3),
                vmix,
                jnp.swapaxes(send_rows, 2, 3),
            )
        )
    )
    return pl.pallas_call(
        finish,
        out_shape=(
            jax.ShapeDtypeStruct((1, LEV, ROWS, COLS), F32),
            jax.ShapeDtypeStruct((VECS,), F32),
        ),
        in_specs=[vmem] * 3,
        out_specs=(pl.BlockSpec(memory_space=pl.ANY),) * 2,
        scratch_shapes=[pltpu.VMEM((LEV, ROWS, COLS), F32), pltpu.VMEM((VECS,), F32), dma(()), dma(())],
        compiler_params=pltpu.CompilerParams(vmem_limit_bytes=16 << 20),
        name="finish",
    )(x2, wide, result)


def solution(mesh):
    return jax.shard_map(
        body,
        mesh=mesh,
        in_specs=(
            P("comp", None, "tile", None),
            P(None, "comp", None, "tile", None),
            P("comp", "tile", None),
            P("comp", None, None),
            P("tile", None),
            P("comp", "tile", None, None),
            P("comp", "tile", None, None),
            P("comp", "tile", None, None),
        ),
        out_specs=(P("comp", None, "tile", None), P()),
        check_vma=False,
    )
```

```python
import functools

import jax
import jax.numpy as jnp
from jax import lax
from jax.experimental import pallas as pl
from jax.experimental.pallas import tpu as pltpu
from jax.sharding import PartitionSpec as P

FLUX = 4
VECS = 12
LEV = 8
ROWS = 16
COLS = 1024
TILES = 64
CAP = 8
NB = 128
GROUPS = 4
PER = TILES // GROUPS
EARLY = 48
MESH = pl.DeviceIdType.MESH
F32 = jnp.float32
BF16 = jnp.bfloat16
SEG = 16


def hops(k):
    return sum((0, 1, 2, 1)[(k >> s) & 3] for s in (0, 2, 4))


FAR_FIRST = sorted(range(TILES), key=lambda k: -hops(k))


FAR = [k for k in FAR_FIRST if hops(k) >= 5]
NEAR = [k for k in FAR_FIRST if 0 < hops(k) < 5]


def offset_of(step):
    a, b, c = step & 3, (step >> 2) & 3, step >> 4
    return a, (b - a) & 3, (a + c) & 3


def moved_tile(tile, step):
    dx, dy, dz = offset_of(step)
    return ((tile & 3) + dx & 3) | (((tile >> 2 & 3) + dy & 3) << 2) | (((tile >> 4) + dz & 3) << 4)


def remote(src, dst, send, recv, comp, tile):
    return pltpu.make_async_remote_copy(
        src_ref=src, dst_ref=dst, send_sem=send, recv_sem=recv, device_id=(comp, tile), device_id_type=MESH
    )


def wait_bytes(ref, sem):
    pltpu.make_async_copy(ref, ref, sem).wait()


def sum_over_devices(comp, tile, mine, pair, chip, far, near, sems, meanwhile):
    first = remote(mine, pair, sems.at[0], sems.at[1], 1 - comp, tile)
    first.start()
    for i, k in enumerate(FAR):
        for c in (0, 1):
            remote(mine, far.at[pl.ds(2 * i + comp, 1)], sems.at[2], sems.at[3], c, tile ^ k).start()
    first.wait()
    chip[...] = mine[...] + pair[...]
    own = pl.ds(tile, 1)
    for core in (0, 1):

        @pl.when(comp == core)
        def _():
            for k in NEAR[core::2]:
                for c in (0, 1):
                    remote(chip, near.at[own], sems.at[4], sems.at[5], c, tile ^ k).start()

    near[own] = chip[...]
    meanwhile()
    wait_bytes(far.at[pl.ds(0, 2 * len(FAR))], sems.at[3])
    for i, k in enumerate(FAR):
        near[pl.ds(tile ^ k, 1)] = far[2 * i : 2 * i + 1] + far[2 * i + 1 : 2 * i + 2]
    wait_bytes(near.at[pl.ds(0, len(NEAR))], sems.at[5])
    total = jnp.sum(near[...], axis=0, keepdims=True)
    return total


def wait_sums(far, near, sems):
    wait_bytes(far.at[pl.ds(0, 2 * len(FAR))], sems.at[2])
    wait_bytes(near.at[pl.ds(0, len(NEAR))], sems.at[4])


def stencil(ref, level, kap):
    x = ref[level, 8:24, :]
    lap = (
        ref[level, 7:23, :]
        + ref[level, 9:25, :]
        + pltpu.roll(x, 1, 1)
        + pltpu.roll(x, COLS - 1, 1)
        - 4.0 * x
    )
    return x + kap * lap


def mixed(ref, vmix, level, terms):
    total = vmix[level, 0] * ref[0, 8:24, :]
    for m in range(1, terms):
        total = total + vmix[level, m] * ref[m, 8:24, :]
    return total


def kernel(
    state, basis, kappa, land, slots_hbm, weights_hbm, vmix_hbm, rows_hbm,
    x2, wide, result,
    slots, weights, vmix, rows, x0, x1, fh, f, kap, land_v, maskf, gram_v, edge_x,
    basis_v, surf, bucket, arrived, imp, edge_b, edge_out, edge_in, edge_k, edge_m, near,
    e_mine, e_pair, e_chip, e_far, e_near,
    load, send, recv, halo, esem,
):
    comp = lax.axis_index("comp")
    tile = lax.axis_index("tile")
    total = float(LEV * ROWS * COLS * TILES * 2)
    above = tile - 1 & TILES - 1
    below = tile + 1 & TILES - 1
    every = range(8)

    barrier = pltpu.get_barrier_semaphore()

    def greet(ks):
        for k in ks:
            pl.semaphore_signal(barrier, inc=1, device_id=(1 - comp, tile ^ k), device_id_type=MESH)

    surf_loads = [
        pltpu.make_async_copy(
            state.at[0, pl.ds(0, FLUX), :, pl.ds(128 * j, 128)], surf.at[j], load.at[0]
        )
        for j in every
    ]
    rows_load = pltpu.make_async_copy(rows_hbm.at[0, 0], rows, load.at[5])
    x_load = pltpu.make_async_copy(state.at[0], x0.at[:, pl.ds(8, ROWS), :], load.at[1])
    greet(FAR_FIRST)
    for t in (above, below):
        pl.semaphore_signal(barrier, inc=1, device_id=(comp, t), device_id_type=MESH)
    for c in [rows_load, *surf_loads]:
        c.start()
    x_load.start()
    kap_load = pltpu.make_async_copy(kappa.at[0], kap, load.at[2])
    kap_load.start()
    land_load = pltpu.make_async_copy(land, land_v, load.at[3])
    land_load.start()
    vmix_load = pltpu.make_async_copy(vmix_hbm.at[0], vmix, load.at[6])
    vmix_load.start()
    table_loads = [
        pltpu.make_async_copy(slots_hbm.at[0, 0], slots, load.at[7]),
        pltpu.make_async_copy(weights_hbm.at[0, 0], weights, load.at[8]),
    ]
    for c in table_loads:
        c.start()
    basis_load = pltpu.make_async_copy(basis.at[:, 0], basis_v, load.at[4])
    rows_load.wait()
    x_load.wait()
    for c in surf_loads:
        c.wait()
    pl.semaphore_wait(barrier, TILES + 2)

    def when_above(f):
        pl.when(tile > 0)(f)

    def when_below(f):
        pl.when(tile < TILES - 1)(f)

    def start_pair(up, down):
        when_above(up.start)
        when_below(down.start)
        return up, down

    def wait_pair(up, down):
        when_below(up.wait_recv)
        when_above(down.wait_recv)
        when_above(up.wait_send)
        when_below(down.wait_send)

    def swap_rows(ref, sems):
        return start_pair(
            remote(ref.at[:, pl.ds(8, 1), :], ref.at[:, pl.ds(24, 1), :], sems.at[0], sems.at[1], comp, above),
            remote(ref.at[:, pl.ds(23, 1), :], ref.at[:, pl.ds(7, 1), :], sems.at[2], sems.at[3], comp, below),
        )

    def clear_ends(ref):
        n = ref.shape[0]

        @pl.when(tile == 0)
        def _():
            ref[:, 7:8, :] = jnp.zeros((n, 1, COLS), F32)

        @pl.when(tile == TILES - 1)
        def _():
            ref[:, 24:25, :] = jnp.zeros((n, 1, COLS), F32)

    swap = swap_rows(x0, halo.at[0])

    flat_surf = surf.reshape(8 * FLUX * ROWS, 128)
    flat_bucket = bucket.reshape(TILES * FLUX * CAP, 128)

    def deliver(step, carry):
        dest = moved_tile(tile, step)
        for j in range(CAP):
            blk = rows[j, dest]
            start = (blk & 7) * (FLUX * ROWS) + (blk >> 3)
            flat_bucket[pl.ds(step * (FLUX * CAP) + j, FLUX, stride=CAP), :] = flat_surf[
                pl.ds(start, FLUX, stride=ROWS), :
            ]
        remote(bucket.at[step], arrived.at[step], send, recv.at[step >> 4], 1 - comp, dest).start()
        return carry

    basis_load.start()
    lax.fori_loop(0, EARLY, deliver, 0)

    vmix_load.wait()
    kap_load.wait()
    land_load.wait()
    maskf[...] = jnp.where(comp == 0, land_v[...].astype(F32), jnp.ones((ROWS, COLS), F32))
    wait_pair(*swap)
    clear_ends(x0)
    for l in range(LEV):
        x1[l, 8:24, :] = maskf[...] * (stencil(x0, l, kap[...]) + mixed(x0, vmix, l, LEV))
    deep = x1.at[pl.ds(FLUX, LEV - FLUX)]
    for row in (7, 24):
        x1[0:FLUX, row : row + 1, :] = jnp.zeros((FLUX, 1, COLS), F32)
        fh[:, row : row + 1, :] = jnp.zeros((FLUX, 1, COLS), F32)
    swap = swap_rows(deep, halo.at[1])
    lax.fori_loop(EARLY, TILES, deliver, 0)

    for j in every:
        cut = slice(j * 128, (j + 1) * 128)
        for end, row in ((0, 0), (1, 15)):
            m = maskf[row : row + 1, cut]
            edge_m[end, j : j + 1] = m
            edge_k[end, j : j + 1] = m * kap[row : row + 1, cut]
            for l in range(FLUX):
                edge_x[end, l, j : j + 1] = x1[l, 8 + row : 9 + row, cut]
    for l in range(FLUX):
        x2[l] = maskf[...] * (stencil(x1, l, kap[...]) + mixed(x1, vmix, l, LEV))

    for c in table_loads:
        c.wait()
    slot = slots[...]
    src = slot >> 3
    a = (tile & 3) - (src & 3) & 3
    b = (tile >> 2 & 3) - (src >> 2 & 3) + a & 3
    c = (tile >> 4) - (src >> 4) - a & 3
    place = (a | b << 2 | c << 4) * CAP + (slot & 7)
    table = jnp.concatenate([place.astype(F32), weights[...], jnp.zeros((NB - 8, NB), F32)], axis=0).T
    at_lane = lax.broadcasted_iota(jnp.int32, (NB, TILES * CAP), 1).astype(F32)
    matrix = jnp.zeros((NB, TILES * CAP), F32)
    for k in range(4):
        matrix = matrix + jnp.where(at_lane == table[:, k : k + 1], table[:, 4 + k : 5 + k], 0.0)
    ends = jnp.concatenate([matrix[:8], matrix[-8:]], axis=0)

    def halves(v):
        high = v.astype(BF16)
        return high, (v - high.astype(F32)).astype(BF16)

    high, low = halves(matrix)
    ends_high, ends_low = halves(ends)

    basis_load.wait()
    lane = lax.broadcasted_iota(jnp.int32, (SEG, 128), 1)
    sub = lax.broadcasted_iota(jnp.int32, (SEG, 128), 0)

    def gram_step(n, acc):
        level = n >> 2
        at = pl.multiple_of((n & 3) * 256, 256)
        x = jnp.concatenate([basis_v[i, level, :, pl.ds(at, 256)] for i in range(VECS)], axis=0)
        gram_v[...] += lax.dot_general(x, x, (((1,), (1,)), ((), ())), preferred_element_type=F32)
        return acc

    span = VECS * ROWS
    gram_v[...] = jnp.zeros((span, span), F32)
    lax.fori_loop(0, 32, gram_step, 0)
    row_of = lax.broadcasted_iota(jnp.int32, (ROWS, span), 0)
    col_of = lax.broadcasted_iota(jnp.int32, (ROWS, span), 1)
    diagonal = row_of == (col_of & ROWS - 1)
    picked = [
        jnp.sum(jnp.where(diagonal, gram_v[i * ROWS : (i + 1) * ROWS, :], 0.0), axis=0, keepdims=True)
        for i in range(VECS)
    ]
    picked = jnp.concatenate(picked + [jnp.zeros((SEG - VECS, span), F32)], axis=0)
    gather = lax.broadcasted_iota(jnp.int32, (span, 128), 0) >> 4 == lax.broadcasted_iota(jnp.int32, (span, 128), 1)
    square = jnp.dot(picked, gather.astype(F32), precision=lax.Precision.HIGHEST, preferred_element_type=F32)
    empty = jnp.zeros((1, 128), F32)

    def to_lanes(rows_, k):
        stack = jnp.concatenate(rows_ + [empty] * (SEG - len(rows_)), axis=0)
        return jnp.where(lane == sub + SEG * k, jnp.sum(stack, axis=1, keepdims=True), 0.0)

    gram = jnp.zeros((SEG, 128), F32)
    for k in range(VECS // 2 + 1):
        other = jnp.where(sub + k >= VECS, sub + k - VECS, sub + k)
        own = sub < (VECS if k < VECS // 2 else VECS // 2)
        col = jnp.sum(jnp.where((lane == other) & own, square, 0.0), axis=1, keepdims=True)
        gram = gram + jnp.where(lane == sub + SEG * k, col, 0.0)

    wait_pair(*swap)
    clear_ends(deep)
    for l in range(FLUX, LEV):
        x2[l] = maskf[...] * (stencil(x1, l, kap[...]) + mixed(x1, vmix, l, LEV))

    def edge_step(i, carry):
        for l in range(FLUX):
            for j in every:
                v = basis_v[i, l, :, j * 128 : (j + 1) * 128].astype(F32)
                edge_b[i, l, 0, j : j + 1] = v[:1]
                edge_b[i, l, 1, j : j + 1] = v[15:]
        return carry

    lax.fori_loop(0, VECS, edge_step, 0)

    dot = functools.partial(jnp.dot, preferred_element_type=F32)

    def group(g):
        wait_bytes(arrived.at[pl.ds(g * PER, PER)], recv.at[g])
        got = jnp.concatenate(
            [arrived[g * PER : (g + 1) * PER, i].reshape(PER * CAP, 128) for i in range(FLUX)], axis=1
        )
        return slice(g * PER * CAP, (g + 1) * PER * CAP), *halves(got)

    def times(high, low, cut, got_high, got_low):
        return dot(high[:, cut], got_high) + dot(low[:, cut], got_high) + dot(high[:, cut], got_low)

    sums = jnp.zeros((NB, FLUX * 128), F32)
    for g in range(GROUPS - 1):
        sums = sums + times(high, low, *group(g))
    tail = group(GROUPS - 1)
    border = jnp.concatenate([sums[:8], sums[-8:]], axis=0) + times(ends_high, ends_low, *tail)
    for end in (0, 1):
        for i in range(FLUX):
            edge_out[end, i] = edge_x[end, i] + edge_m[end] * border[end * 8 : end * 8 + 8, i * 128 : (i + 1) * 128]
    edges = start_pair(
        remote(edge_out.at[0], edge_in.at[1], halo.at[2, 0], halo.at[2, 1], comp, above),
        remote(edge_out.at[1], edge_in.at[0], halo.at[2, 2], halo.at[2, 3], comp, below),
    )
    sums = sums + times(high, low, *tail)
    for i in range(FLUX):
        imp[i * NB : (i + 1) * NB, :] = sums[:, i * 128 : (i + 1) * 128]
    for i in range(FLUX):
        for j in every:
            cut = slice(j * 128, (j + 1) * 128)
            piece = imp[pl.ds(i * NB + j, ROWS, stride=8), :]
            f[i, :, cut] = piece
            fh[i, 8:24, cut] = maskf[:, cut] * piece
    for l in range(LEV):
        z = mixed(fh, vmix, l, FLUX)
        if l < FLUX:
            z = z + stencil(fh, l, kap[...]) + f[l]
        x2[l] = x2[l] + maskf[...] * z

    def dot_step(n, acc):
        level = n >> 2
        for half in (0, 1):
            at = pl.multiple_of((n & 3) * 256 + half * 128, 128)
            x = x2[level, :, pl.ds(at, 128)]
            out = [a + basis_v[i, level, :, pl.ds(at, 128)].astype(F32) * x for i, a in enumerate(acc[:VECS])]
            acc = tuple(out) + (acc[VECS] + x * x,)
        return acc

    acc = lax.fori_loop(0, 32, dot_step, tuple(jnp.zeros((16, 128), F32) for _ in range(VECS + 1)))
    acc = [a[:8] + a[8:] for a in acc]
    for l in range(FLUX):
        for end, row in ((0, 0), (1, 15)):
            for j in every:
                near[l, end, j : j + 1] = x2[l, row : row + 1, j * 128 : (j + 1) * 128]
    wait_pair(*edges)
    extra = {}
    for end, last in ((0, 0), (1, TILES - 1)):
        for l in range(FLUX):
            add = jnp.where(tile == last, jnp.zeros((8, 128), F32), edge_k[end] * edge_in[end, l])
            extra[l, end] = add
            for i in range(VECS):
                acc[i] = acc[i] + edge_b[i, l, end] * add
            acc[VECS] = acc[VECS] + add * (2.0 * near[l, end] + add)
    sums_of = [jnp.sum(a, axis=0, keepdims=True) for a in acc]
    e_mine[...] = jnp.sum(gram + to_lanes(sums_of, 7), axis=0, keepdims=True)

    def widen(i, carry):
        for l in range(LEV):
            wide[i, l] = basis_v[i, l].astype(F32)
        return carry

    def add_edges():
        lax.fori_loop(0, VECS, widen, 0)
        for (l, end), add in extra.items():
            row = 15 * end
            full = near[l, end] + add
            for j in every:
                x2[l, row : row + 1, j * 128 : (j + 1) * 128] = full[j : j + 1]

    dots = sum_over_devices(comp, tile, e_mine, e_pair, e_chip, e_far, e_near, esem, add_edges)

    one = lax.broadcasted_iota(jnp.int32, (1, 128), 1)
    seg, pos = one >> 4, one & 15
    vals = jnp.where((seg == 7) & (pos < VECS), dots * (1.0 / total), 0.0)
    coef = pltpu.roll(vals, SEG, 1)
    twice = coef + pltpu.roll(coef, VECS, 1)
    left = jnp.zeros((1, 128), F32)
    right = jnp.zeros((1, 128), F32)
    for k in range(VECS // 2 + 1):
        left = jnp.where(seg == k, pltpu.roll(coef, SEG * k, 1) if k else coef, left)
        right = jnp.where(seg == k, pltpu.roll(twice, (SEG - 1) * k, 1) if k else twice, right)
    factor = jnp.where(seg == 0, 1.0, 2.0)
    products = jnp.where((seg < 7) & (pos < VECS), factor * dots * left * right, 0.0)
    square = jnp.where((seg == 7) & (pos == VECS), dots, 0.0) - 2.0 * dots * vals + products
    square = jnp.sum(square, axis=1, keepdims=True)
    scale = 1.0 / jnp.sqrt(jnp.maximum(square, 0.0) * (1.0 / total) + 1e-06)
    line = jnp.where(one == VECS, 1.0, coef)
    column = jnp.sum(jnp.where(lane == sub, jnp.broadcast_to(line, (SEG, 128)), 0.0), axis=1, keepdims=True)
    result[0:SEG] = jnp.broadcast_to(column * scale, (SEG, 128))
    result[SEG : SEG + 1] = coef
    wait_sums(e_far, e_near, esem)
    wait_bytes(bucket, send)


def finish(x2, wide, result, direction, coefs, out, line, store, small):
    line[...] = result[SEG, :VECS]
    first = pltpu.make_async_copy(line, coefs, small)
    first.start()
    weigh = [jnp.broadcast_to(result[i : i + 1], (ROWS, 128)) for i in range(VECS + 1)]
    for l in range(LEV):

        def part(n, carry):
            for half in (0, 1):
                at = n * 256 + half * 128
                w = weigh[VECS] * x2[l, :, pl.ds(at, 128)]
                for i in range(VECS):
                    w = w - weigh[i] * wide[i, l, :, pl.ds(at, 128)]
                out[l, :, pl.ds(at, 128)] = w
            return carry

        for n in range(4):
            part(n, 0)
        pltpu.make_async_copy(out.at[l], direction.at[0, l], store).start()
    first.wait()
    wait_bytes(out, store)


def body(state, basis, kappa, vmix, land_mask, send_rows, recv_slots, recv_weights):
    vmem = pl.BlockSpec(memory_space=pltpu.VMEM)
    dma = pltpu.SemaphoreType.DMA
    pad = (LEV, 32, COLS)
    band = (ROWS, COLS)
    ints = jnp.int32
    scratch = [((4, NB), ints), ((4, NB), F32), None, None, (pad, F32), (pad, F32)]
    scratch += [((FLUX, 32, COLS), F32), ((FLUX, ROWS, COLS), F32), (band, F32), (band, ints), (band, F32)]
    scratch += [((VECS * ROWS, VECS * ROWS), F32), ((2, FLUX, 8, 128), F32)]
    scratch += [((VECS, LEV, ROWS, COLS), BF16), ((8, FLUX, ROWS, 128), F32)]
    scratch += [((TILES, FLUX, CAP, 128), F32)] * 2 + [((FLUX * NB, 128), F32)]
    scratch += [((VECS, FLUX, 2, 8, 128), F32)] + [((2, FLUX, 8, 128), F32)] * 2 + [((2, 8, 128), F32)] * 2
    scratch += [((FLUX, 2, 8, 128), F32)]
    scratch += [((1, 128), F32)] * 3 + [((16, 128), F32), ((TILES, 128), F32)]
    scratch = [pltpu.VMEM(*v) if v else None for v in scratch]
    scratch[2] = pltpu.SMEM((LEV, LEV), F32)
    scratch[3] = pltpu.SMEM((CAP, TILES), ints)
    x2, wide, result = pl.pallas_call(
        kernel,
        out_shape=(
            jax.ShapeDtypeStruct((LEV, ROWS, COLS), F32),
            jax.ShapeDtypeStruct((VECS, LEV, ROWS, COLS), F32),
            jax.ShapeDtypeStruct((SEG + 8, 128), F32),
        ),
        in_specs=[pl.BlockSpec(memory_space=pltpu.HBM)] * 8,
        out_specs=(vmem,) * 3,
        scratch_shapes=scratch + [dma((9,)), dma(()), dma((GROUPS,)), dma((3, 4)), dma((6,))],
        compiler_params=pltpu.CompilerParams(
            collective_id=0, has_side_effects=True, vmem_limit_bytes=24 << 20
        ),
        name="interval",
    )(
        *(
            pltpu.with_memory_space_constraint(v, pltpu.HBM)
            for v in (
                state,
                basis,
                kappa,
                land_mask,
                jnp.swapaxes(recv_slots, 2, 3),
                jnp.swapaxes(recv_weights, 2, 3),
                vmix,
                jnp.swapaxes(send_rows, 2, 3),
            )
        )
    )
    return pl.pallas_call(
        finish,
        out_shape=(
            jax.ShapeDtypeStruct((1, LEV, ROWS, COLS), F32),
            jax.ShapeDtypeStruct((VECS,), F32),
        ),
        in_specs=[vmem] * 3,
        out_specs=(pl.BlockSpec(memory_space=pl.ANY),) * 2,
        scratch_shapes=[pltpu.VMEM((LEV, ROWS, COLS), F32), pltpu.VMEM((VECS,), F32), dma(()), dma(())],
        compiler_params=pltpu.CompilerParams(vmem_limit_bytes=16 << 20),
        name="finish",
    )(x2, wide, result)


def solution(mesh):
    return jax.shard_map(
        body,
        mesh=mesh,
        in_specs=(
            P("comp", None, "tile", None),
            P(None, "comp", None, "tile", None),
            P("comp", "tile", None),
            P("comp", None, None),
            P("tile", None),
            P("comp", "tile", None, None),
            P("comp", "tile", None, None),
            P("comp", "tile", None, None),
        ),
        out_specs=(P("comp", None, "tile", None), P()),
        check_vma=False,
    )
```
